32 devices in a mesh: basin: 2 (over x), dom: 8 (over z, y), hid: 2 (over core).
Axes of the slice: x: 2, y: 2, z: 4, core: 2. Of those that a mesh axis runs over, the one named last changes fastest.
Arguments:
- feats: bfloat16 [32768, 512], P(('basin', 'dom'), 'hid'), parts along dimension 0, may hold values from -6 to 6
- tiles: bfloat16 [256, 16, 128, 128], P(('basin', 'dom')), parts along dimension 0, may hold values from -0.125 to 0.125
- tile_cols: int32 [256, 16], P(('basin', 'dom')), parts along dimension 0, may hold values from 0 to 39, as said below
- sends: int32 [16, 3, 8], P(('basin', 'dom')), parts along dimension 0, may hold values from 0 to 15, as said below
- pins: int32 [16, 32], P(('basin', 'dom')), parts along dimension 0, may hold values from 0 to 2047, as said below
- weight: bfloat16 [512, 512], P(None, 'hid'), may hold values from -0.25 to 0.25
- bias: float32 [512], P('hid'), may hold values from -3 to 3
- cotan: bfloat16 [32768, 512], P(('basin', 'dom'), 'hid'), parts along dimension 0, may hold values from -6 to 6
Outputs:
- out: bfloat16 [32768, 512], P(('basin', 'dom'), 'hid'), parts along dimension 0
- dfeat: bfloat16 [32768, 512], P(('basin', 'dom'), 'hid'), parts along dimension 0
- dweight: float32 [1024, 512], P('basin', 'hid'), parts along dimension 0
- dbias: float32 [1024], P(('basin', 'hid')), parts along dimension 0
The draws below stay inside these ranges and needn't reach their ends.
There are 2 independent parts, one for each index of `basin`. The reference program is written for one: setup_inputs(seed, part) draws one part's arguments, and reference() takes and returns one part's arrays. A program takes and returns all parts, laid end to end along the dimension named above; an argument that names none is the same for every part. Nothing has to cross between parts.
Inputs may be any that keep to these rules, and one draw needn't show every extreme that they name: `tile_cols`: every one of a partition's 40 sources is read by at least one of its tiles. `sends`: within one partition and matching the entries are distinct; every owned block of a partition is sent in some matching. `pins`: entries may repeat.
All inputs are finite; a program needn't handle non-finite values.
Results may differ from the reference program's by a relative error of at most 0.0054.
Values may be sent and summed in bfloat16 or wider, within the bound.
A program may use at most 128 MiB of HBM per device.

```python
import math
import jax
import jax.numpy as jnp
from jax import lax

H = 512
VERT_DEV = 2048
K = 16
PINS = 32
BLOCKS_DEV = 16
SEND_BLOCKS = 8
SOURCES = 40
VERTS = 16384
RBLK = 128
N_DOM = 8


def draw_tile_cols(key, part):
    slots = BLOCKS_DEV * K

    def one_part(sub):
        first, second, third = jax.random.split(sub, 3)
        base = jax.random.permutation(first, SOURCES)
        extra = jax.random.randint(second, (slots - SOURCES,), 0, SOURCES)
        return jax.random.permutation(third, jnp.concatenate([base, extra]))
    keys = jax.random.split(jax.random.fold_in(key, 11), N_DOM)
    return jax.vmap(one_part)(keys).reshape(N_DOM * BLOCKS_DEV, K).astype(jnp.int32)


def draw_sends(key, part):
    keys = jax.random.split(jax.random.fold_in(key, 3), N_DOM)
    slot = (jnp.arange(3)[:, None] * SEND_BLOCKS + jnp.arange(SEND_BLOCKS)[None, :]) % BLOCKS_DEV
    return jax.vmap(lambda sub: jax.random.permutation(sub, BLOCKS_DEV)[slot])(keys).astype(jnp.int32)


def draw_pins(key, part):
    first, second = jax.random.split(jax.random.fold_in(key, 7))
    keys = jax.random.split(first, N_DOM)
    ids = jax.vmap(lambda sub: jax.random.permutation(sub, VERT_DEV)[:PINS])(keys)
    chosen = jax.random.randint(second, (), 0, N_DOM)
    rowsel = jnp.arange(N_DOM)[:, None] == chosen
    colsel = jnp.arange(PINS)[None, :]
    ends = jnp.where(colsel == 0, 0, VERT_DEV - 1)
    fixed = rowsel & (colsel < 2)
    return jnp.where(fixed, ends, ids).astype(jnp.int32)


def level_of(key, dims, shards, low, top_value):
    level = 1.0
    for axis_at, blocks in shards:
        steps = jax.random.uniform(jax.random.fold_in(jax.random.fold_in(key, 6), axis_at), (blocks,), jnp.float32, low / len(shards), top_value / len(shards))
        level = level * jnp.repeat(jnp.exp(steps), dims[axis_at] // blocks).reshape((-1,) + (1,) * (len(dims) - 1 - axis_at))
    return level


def normal_values(own_key, dims, deviation, most, shards=(), held_as=jnp.bfloat16):
    factor_of = level_of(own_key, dims, shards, -0.22, 0.18) if shards else 1.0
    values = jax.random.normal(own_key, dims, jnp.float32) * deviation * factor_of
    return jnp.minimum(jnp.maximum(values, -most), most).astype(held_as)


def setup_inputs(seed: int = 0, part: int = 0) -> dict:
    arg_keys = jax.random.split(jax.random.key(seed), 9)
    part_splits = jax.random.split(jax.random.fold_in(arg_keys[8], part), 9)
    feats = normal_values(part_splits[0], (VERTS, H), 1.0, 6.0, ((0, 8), (1, 2)))
    tiles = normal_values(part_splits[1], (RBLK, K, 128, 128), (128 * K) ** -0.5, 0.125, ((0, 8),))
    tile_cols = draw_tile_cols(jax.random.fold_in(jax.random.fold_in(arg_keys[8], part), 71), part)
    sends = draw_sends(jax.random.fold_in(jax.random.fold_in(arg_keys[8], part), 71), part)
    pins = draw_pins(jax.random.fold_in(jax.random.fold_in(arg_keys[8], part), 71), part)
    weight = normal_values(arg_keys[5], (H, H), H ** -0.5, 0.25, ((1, 2),))
    bias = normal_values(arg_keys[6], (H,), 0.5, 3.0, ((0, 2),), jnp.float32)
    cotan = normal_values(part_splits[7], (VERTS, H), 1.0, 6.0, ((0, 8), (1, 2)))
    return {"feats": feats, "tiles": tiles, "tile_cols": tile_cols, "sends": sends, "pins": pins, "weight": weight, "bias": bias, "cotan": cotan}


def partners(shift):
    return jnp.bitwise_xor(jnp.arange(N_DOM, dtype=jnp.int32), jnp.int32(1 << shift))

def reference(feats, tiles, tile_cols, sends, pins, weight, bias, cotan):
    nbits = N_DOM.bit_length() - 1
    shifts = (0, nbits // 2, nbits - 1)
    blocks = feats.reshape(N_DOM, BLOCKS_DEV, 128, H)
    tile_dev = tiles.reshape(N_DOM, BLOCKS_DEV, K, 128, 128)
    cols_dev = tile_cols.reshape(N_DOM, BLOCKS_DEV, K)
    received = []
    for m in range(3):
        mate = partners(shifts[m])
        chosen = jax.vmap(lambda one, idx: one[idx])(blocks, sends[:, m, :])
        received.append(chosen[mate])
    sources = jnp.concatenate([blocks] + received, axis=1)

    def aggregate(items):
        tile_one, cols_one, src_one = items
        picked = src_one[cols_one]
        return jnp.einsum('rkij,rkjh->rih', tile_one.astype(jnp.float32), picked.astype(jnp.float32))
    agg = lax.map(aggregate, (tile_dev, cols_dev, sources)).astype(jnp.bfloat16).reshape(VERTS, H)
    pre = jnp.dot(agg, weight, preferred_element_type=jnp.float32) + bias
    local_ids = jnp.arange(VERT_DEV, dtype=jnp.int32)
    pinned = jnp.any(local_ids[None, :, None] == pins[:, None, :], axis=2).reshape(VERTS)
    keep = 1.0 - pinned.astype(jnp.float32)
    sig = jax.nn.sigmoid(pre)
    out = (feats.astype(jnp.float32) + keep[:, None] * pre * sig).astype(jnp.bfloat16)
    dpre = (keep[:, None] * cotan.astype(jnp.float32) * sig * (1.0 + pre * (1.0 - sig))).astype(jnp.bfloat16)
    scale = 1.0 / math.sqrt(VERTS)
    dweight = jnp.dot(agg.T, dpre, preferred_element_type=jnp.float32) * scale
    dbias = lax.optimization_barrier(jnp.sum(dpre.astype(jnp.float32), axis=0)) * scale
    dagg = jnp.dot(dpre, weight.T, preferred_element_type=jnp.float32).astype(jnp.bfloat16)
    dblocks = dagg.reshape(N_DOM, BLOCKS_DEV, 128, H)

    def spread(items):
        tile_one, cols_one, grad_one = items
        prod = jnp.einsum('rkij,rih->rkjh', tile_one.astype(jnp.float32), grad_one.astype(jnp.float32))
        onehot = (cols_one.reshape(-1)[:, None] == jnp.arange(SOURCES, dtype=jnp.int32)[None, :]).astype(jnp.float32)
        return jnp.einsum('ns,njh->sjh', onehot, prod.reshape(BLOCKS_DEV * K, 128, H), precision=lax.Precision.HIGHEST)
    dsrc = lax.map(spread, (tile_dev, cols_dev, dblocks))
    own = dsrc[:, :BLOCKS_DEV]
    for m in range(3):
        mate = partners(shifts[m])
        back = dsrc[:, BLOCKS_DEV + m * SEND_BLOCKS:BLOCKS_DEV + (m + 1) * SEND_BLOCKS][mate]
        onehot = (sends[:, m, :, None] == jnp.arange(BLOCKS_DEV, dtype=jnp.int32)[None, None, :]).astype(jnp.float32)
        own = own + jnp.einsum('ejr,ejih->erih', onehot, back, precision=lax.Precision.HIGHEST)
    dfeat = (cotan.astype(jnp.float32) + own.reshape(VERTS, H)).astype(jnp.bfloat16)
    return (out, dfeat, dweight, dbias)
```

```python
import functools
import math

import jax
import jax.numpy as jnp
from jax import lax
from jax.experimental import pallas as pl
from jax.experimental.pallas import tpu as pltpu
from jax.sharding import PartitionSpec as P

BLK = 128
LANES = 128
ZQ = 4
CQ = 4
GROUP = 4
VMEM = pltpu.VMEM
F32 = jnp.float32

MESH = pl.DeviceIdType.MESH
SMEM_SPEC = pl.BlockSpec(memory_space=pltpu.SMEM)
VMEM_SPEC = pl.BlockSpec(memory_space=pltpu.VMEM)
ANY_SPEC = pl.BlockSpec(memory_space=pl.ANY)

DEEP = (((0,), (0,)), ((), ()))


def flipped(index, bit):
    return index + (1 - 2 * ((index // (1 << bit)) % 2)) * (1 << bit)


def tables(cols, sends_ref):
    nblock, ntile = cols.shape
    nsend = sends_ref.shape[2]
    lane = lax.broadcasted_iota(jnp.int32, (nblock, LANES), 1)
    row = lax.broadcasted_iota(jnp.int32, (nblock, LANES), 0)
    wide = jnp.concatenate([cols, jnp.full((nblock, LANES - ntile), LANES, jnp.int32)], axis=1)
    one = [jnp.broadcast_to(cols[:, k : k + 1], (nblock, LANES)) for k in range(ntile)]
    rank = jnp.zeros((nblock, LANES), jnp.int32)
    upto = jnp.zeros((nblock, LANES), jnp.int32)
    same = jnp.zeros((nblock, LANES), jnp.int32)
    for k in range(ntile):
        before = (one[k] < wide) | ((one[k] == wide) & (k < lane))
        rank = rank + jnp.where(before, 1, 0)
        upto = upto + jnp.where(one[k] <= lane, 1, 0)
        same = same + jnp.where(one[k] == lane, 1, 0)
    merged = jnp.where(same > 0, row * ntile + upto - 1, nblock * ntile)
    perm = jnp.zeros((nblock, LANES), jnp.int32)
    here = jnp.full((nblock, LANES), -1, jnp.int32)
    prev = jnp.full((nblock, LANES), -2, jnp.int32)
    for k in range(ntile):
        at = jnp.broadcast_to(rank[:, k : k + 1], (nblock, LANES))
        perm = perm + jnp.where(at == lane, row * ntile + k, 0)
        here = jnp.where(at == lane, one[k], here)
        prev = jnp.where(at + 1 == lane, one[k], prev)
    chain = jnp.where(here == prev, 1, 0)
    lanes = lax.broadcasted_iota(jnp.int32, (8, LANES), 1)
    rows = lax.broadcasted_iota(jnp.int32, (8, LANES), 0)
    inverse = jnp.full((8, LANES), nsend, jnp.int32)
    for m in range(3):
        for j in range(nsend):
            inverse = jnp.where((lanes == sends_ref[m, 0, j]) & (rows == m), j, inverse)
    return jnp.concatenate([perm, chain, merged, inverse], axis=0)


def layer_kernel(
    shifts, nbits,
    cols_ref, sends_ref, pins_ref, bias_ref, feats_hbm, tiles_hbm, w_hbm, cotan_hbm,
    out_hbm, dfeat_hbm, dw_hbm, db_ref,
    feats, held, fold, turned, cotan, kcot, keep, w, wx, wt,
    outbox, rz, r0, acc, agg, other, dpre, dother, dagg, outv, dfv,
    bz, b0, in0, in1, in2, wsum, outw, inw, gath, bsum, btmp, dwv, tabv, tab,
    fetch_sem, zsend, zrecv, msend, mrecv, xsend, xrecv, asend, arecv, dsend, drecv,
    bsend, brecv, nsend_sem, nrecv_sem, rsend, rrecv, gsend, grecv, vsend, vrecv, put_sem,
):
    nblock, ntile = cols_ref.shape
    width = feats.shape[2]
    rows = nblock * BLK
    ntiles = nblock * ntile
    high = w.shape[0]
    nsend = sends_ref.shape[2]
    step = nsend // ZQ
    merged = 2 * nblock
    inverse = 3 * nblock
    me = lax.axis_index("dom")
    hid = lax.axis_index("hid")
    peer = 1 - hid

    def wide(start, size):
        return pl.ds(pl.multiple_of(start, 16), size)

    here = wide(hid * width, width)
    there = wide(peer * width, width)

    def remote(src, dst, send, recv, where):
        return pltpu.make_async_remote_copy(
            src_ref=src, dst_ref=dst, send_sem=send, recv_sem=recv,
            device_id=where, device_id_type=MESH,
        )

    def mate(bit):
        return {"dom": flipped(me, bit)}

    get_feats = pltpu.make_async_copy(feats_hbm, feats, fetch_sem.at[0])
    get_tiles = pltpu.make_async_copy(tiles_hbm, held, fetch_sem.at[1])
    get_w = pltpu.make_async_copy(w_hbm, w, fetch_sem.at[2])
    get_cotan = pltpu.make_async_copy(cotan_hbm, cotan, fetch_sem.at[3])
    get_feats.start()

    barrier = pltpu.get_barrier_semaphore()
    for bit in range(nbits):
        pl.semaphore_signal(barrier, inc=1, device_id=mate(bit), device_id_type=MESH)
    pl.semaphore_signal(barrier, inc=1, device_id={"hid": peer}, device_id_type=MESH)
    get_w.start()
    get_tiles.start()
    get_cotan.start()

    def zcopy(m, q):
        part = pl.ds((2 - m) * step * BLK, step * BLK)
        return remote(
            outbox.at[m, pl.ds(q * step * BLK, step * BLK)], rz.at[q, part],
            zsend.at[m - 1, q], zrecv.at[m - 1, q], mate(shifts[m]),
        )

    def mcopy():
        return remote(outbox.at[0], r0, msend, mrecv, mate(shifts[0]))

    get_feats.wait()
    for m in (2, 1, 0):
        for j in range(nsend):
            outbox[m, j * BLK : (j + 1) * BLK] = feats[sends_ref[m, 0, j]]
    get_w.wait()
    pl.semaphore_wait(barrier, nbits + 1)
    for q in range(ZQ):
        zcopy(2, q).start()
        zcopy(1, q).start()
        if q == 0:
            mcopy().start()
    wcopy = remote(w.at[there], wx, xsend, xrecv, {"hid": peer})
    wcopy.start()

    tabv[...] = tables(cols_ref[...], sends_ref)
    get_tab = pltpu.make_async_copy(tabv, tab, fetch_sem.at[4])
    get_tab.start()
    fold[ntiles] = jnp.zeros((BLK, BLK), fold.dtype)
    turned[ntiles] = jnp.zeros((BLK, BLK), turned.dtype)
    for ref in (in0, in1, in2):
        ref[nsend] = jnp.zeros((BLK, width), ref.dtype)
    get_tab.wait()
    get_tiles.wait()

    def fold_row(r, carry):
        total = jnp.zeros((BLK, BLK), F32)
        for n in range(ntile):
            link = tab[nblock + r, n].astype(F32)
            total = total * link + held[tab[r, n]].astype(F32)
            value = total.astype(fold.dtype)
            fold[r * ntile + n] = value
            turned[r * ntile + n] = value.T
        return carry

    lax.fori_loop(0, nblock, fold_row, 0)

    def gathered(i, sources):
        return jnp.concatenate(
            [
                jnp.concatenate([fold[tab[merged + i * GROUP + g, s]] for s in sources], axis=1)
                for g in range(GROUP)
            ],
            axis=0,
        )

    def span_of(i):
        return wide(i * GROUP * BLK, GROUP * BLK)

    def own_part(i, carry):
        acc[span_of(i), :] = jnp.dot(
            gathered(i, range(nblock)), feats[...].reshape(rows, width), preferred_element_type=F32
        )
        return carry

    lax.fori_loop(0, nblock // GROUP, own_part, 0)

    get_cotan.wait()
    chunk = 256

    def keep_part(i, carry):
        span = wide(i * chunk, chunk)
        ids = lax.broadcasted_iota(jnp.int32, (chunk, pins_ref.shape[1]), 0) + i * chunk
        hit = jnp.where(ids == pins_ref[...], 1.0, 0.0)
        kept = jnp.broadcast_to(1.0 - jnp.max(hit, axis=1, keepdims=True), (chunk, LANES))
        keep[span, :] = kept
        both = jnp.concatenate([kept] * (width // LANES), axis=1)
        kcot[span, :] = (cotan[span, :].astype(F32) * both).astype(kcot.dtype)
        return carry

    lax.fori_loop(0, rows // chunk, keep_part, 0)
    wt[0:width] = w[here, :].T
    wcopy.wait()
    wt[width : 2 * width] = wx[...].T

    mcopy().wait()

    def near_part(i, carry):
        acc[span_of(i), :] += jnp.dot(
            gathered(i, range(nblock, nblock + nsend)), r0[...], preferred_element_type=F32
        )
        return carry

    lax.fori_loop(0, nblock // GROUP, near_part, 0)

    def far_sources(q):
        return [nblock + m * nsend + q * step + j for m in (2, 1) for j in range(step)]

    def far_part(q, i):
        return acc[span_of(i), :] + jnp.dot(
            gathered(i, far_sources(q)), rz[q], preferred_element_type=F32
        )

    for q in range(ZQ - 1):
        zcopy(2, q).wait()
        zcopy(1, q).wait()

        def some_part(i, carry, q=q):
            acc[span_of(i), :] = far_part(q, i)
            return carry

        lax.fori_loop(0, nblock // GROUP, some_part, 0)

    part = rows // CQ

    def piece(c):
        return wide(c * part, part)

    def acopy(c):
        return remote(
            agg.at[piece(c)], other.at[piece(c)], asend.at[c], arecv.at[c], {"hid": peer}
        )

    def dcopy(c):
        return remote(
            dpre.at[piece(c)], dother.at[piece(c)], dsend.at[c], drecv.at[c], {"hid": peer}
        )

    def ocopy(c):
        return pltpu.make_async_copy(outv.at[piece(c)], out_hbm.at[piece(c)], put_sem.at[c])

    zcopy(2, ZQ - 1).wait()
    zcopy(1, ZQ - 1).wait()

    def last_part(i, carry):
        agg[span_of(i), :] = far_part(ZQ - 1, i).astype(agg.dtype)
        acopy(i).start()
        return carry

    lax.fori_loop(0, nblock // GROUP, last_part, 0)

    def middle(c, carry):
        acopy(c).wait()

        def inner(i, carry):
            span = wide(c * part + i * chunk, chunk)
            pre = (
                jnp.dot(agg[span, :], w[here, :], preferred_element_type=F32)
                + jnp.dot(other[span, :], w[there, :], preferred_element_type=F32)
                + bias_ref[...]
            )
            both = jnp.concatenate([keep[span, :]] * (width // LANES), axis=1)
            sig = jax.nn.sigmoid(pre)
            gate = pre * sig
            at = pl.ds(c * (part // BLK) + i * (chunk // BLK), chunk // BLK)
            old = feats[at].reshape(chunk, width).astype(F32)
            outv[span, :] = (old + both * gate).astype(outv.dtype)
            dpre[span, :] = (
                kcot[span, :].astype(F32) * (sig * (1.0 + pre * (1.0 - sig)))
            ).astype(dpre.dtype)
            return carry

        lax.fori_loop(0, part // chunk, inner, 0)
        dcopy(c).start()
        ocopy(c).start()
        return carry

    lax.fori_loop(0, CQ, middle, 0)

    def undo(c, carry):
        dcopy(c).wait()
        span = piece(c)
        both = jnp.concatenate([dpre[span, :], dother[span, :]], axis=1)
        dagg[span, :] = jnp.dot(both, wt[...], preferred_element_type=F32).astype(dagg.dtype)
        return carry

    lax.fori_loop(0, CQ, undo, 0)

    def spread(sources):
        lhs = jnp.concatenate(
            [
                jnp.concatenate([turned[tab[merged + r, s]] for r in range(nblock)], axis=1)
                for s in sources
            ],
            axis=0,
        )
        return jnp.dot(lhs, dagg[...], preferred_element_type=F32)

    boxes = {1: in1, 2: in2}

    def bcopy(m, q):
        return remote(
            bz.at[q, pl.ds((2 - m) * step, step)], boxes[m].at[pl.ds(q * step, step)],
            bsend.at[m - 1, q], brecv.at[m - 1, q], mate(shifts[m]),
        )

    def far_back(q, carry):
        bz[q] = spread(far_sources(q)).astype(bz.dtype).reshape(2 * step, BLK, width)
        bcopy(2, q).start()
        bcopy(1, q).start()
        return carry

    lax.fori_loop(0, ZQ, far_back, 0)

    wsum[...] = jnp.zeros_like(wsum)
    bsum[...] = jnp.zeros_like(bsum)

    def deep(c, carry):
        span = piece(c)
        grad = dpre[span, :]
        wsum[here, :] += lax.dot_general(agg[span, :], grad, DEEP, preferred_element_type=F32)
        wsum[there, :] += lax.dot_general(other[span, :], grad, DEEP, preferred_element_type=F32)
        bsum[...] += jnp.sum(grad.astype(F32).reshape(part // 8, 8, width), axis=0)
        return carry

    lax.fori_loop(0, CQ, deep, 0)

    state = {"start": me * 0, "size": high, "at": 0}

    def reduce_start(bit):
        half = state["size"] // 2
        upper = (me // (1 << bit)) % 2
        give = state["start"] + (1 - upper) * half
        state["start"] = state["start"] + upper * half
        state["size"] = half
        at = state["at"]
        outw[at : at + half] = wsum[wide(give, half)].astype(outw.dtype)
        outgoing = bsum if bit == 0 else btmp.at[2 * bit - 1]
        copies = (
            remote(outw.at[pl.ds(at, half)], inw.at[pl.ds(at, half)], rsend.at[bit], rrecv.at[bit], mate(bit)),
            remote(outgoing, btmp.at[2 * bit], vsend.at[bit], vrecv.at[bit], mate(bit)),
        )
        for copy in copies:
            copy.start()
        return copies

    def reduce_end(bit, copies):
        for copy in copies:
            copy.wait()
        half, at = state["size"], state["at"]
        wsum[wide(state["start"], half)] += inw[at : at + half].astype(F32)
        outgoing = bsum[...] if bit == 0 else btmp[2 * bit - 1]
        btmp[2 * bit + 1] = outgoing + btmp[2 * bit]
        state["at"] = at + half
        if bit == nbits - 1:
            span = wide(state["start"], half)
            gath[span] = wsum[span].astype(gath.dtype)

    def gather_start(bit):
        span = wide(state["start"], state["size"])
        copy = remote(gath.at[span], gath.at[span], gsend.at[bit], grecv.at[bit], mate(bit))
        copy.start()
        return (copy,)

    def gather_end(bit, copies):
        for copy in copies:
            copy.wait()
        state["start"] = state["start"] - ((me // (1 << bit)) % 2) * state["size"]
        state["size"] = state["size"] * 2

    stages = [(reduce_start, reduce_end, bit) for bit in range(nbits)]
    stages += [(gather_start, gather_end, bit) for bit in reversed(range(nbits))]
    flying = stages[0][0](stages[0][2])

    def near_back(i, carry):
        sources = [nblock + i * GROUP + g for g in range(GROUP)]
        b0[pl.ds(i * GROUP, GROUP)] = spread(sources).astype(b0.dtype).reshape(GROUP, BLK, width)
        return carry

    lax.fori_loop(0, nsend // GROUP, near_back, 0)
    ncopy = remote(b0, in0.at[pl.ds(0, nsend)], nsend_sem, nrecv_sem, mate(shifts[0]))
    ncopy.start()

    def own_back(i, carry):
        span = span_of(i)
        acc[span, :] = cotan[span, :].astype(F32) + spread([i * GROUP + g for g in range(GROUP)])
        return carry

    lax.fori_loop(0, nblock // GROUP, own_back, 0)

    for i in range(len(stages)):
        stages[i][1](stages[i][2], flying)
        if i + 1 < len(stages):
            flying = stages[i + 1][0](stages[i + 1][2])
    scale = 1.0 / math.sqrt((1 << nbits) * rows)
    dwv[...] = gath[...].astype(F32) * scale
    put_dw = pltpu.make_async_copy(dwv, dw_hbm, put_sem.at[CQ])
    put_dw.start()
    db_ref[...] = jnp.sum(btmp[2 * nbits - 1], axis=0, keepdims=True) * scale

    ncopy.wait()
    for q in range(ZQ):
        bcopy(2, q).wait()
        bcopy(1, q).wait()

    def join(b, carry):
        span = wide(b * BLK, BLK)
        total = acc[span, :]
        for m, ref in enumerate((in0, in1, in2)):
            total = total + ref[tab[inverse + m, b]].astype(F32)
        dfv[span, :] = total.astype(dfv.dtype)
        return carry

    lax.fori_loop(0, nblock, join, 0)
    put_df = pltpu.make_async_copy(dfv, dfeat_hbm, put_sem.at[CQ + 1])
    put_df.start()
    for c in range(CQ):
        ocopy(c).wait()
    put_dw.wait()
    put_df.wait()


def layer_call(cols, sends, pins, bias, feats, tiles, weight, cotan, shifts, nbits):
    rows, width = feats.shape
    nblock, ntile = cols.shape
    ntiles = nblock * ntile
    high = weight.shape[0]
    nsend = sends.shape[2]
    step = nsend // ZQ
    blocks = feats.reshape(nblock, BLK, width)
    sem = pltpu.SemaphoreType.DMA
    half = feats.dtype
    flat = VMEM((rows, width), half)
    square = VMEM((high, width), half)
    return pl.pallas_call(
        functools.partial(layer_kernel, shifts, nbits),
        in_specs=[VMEM_SPEC, SMEM_SPEC, VMEM_SPEC, VMEM_SPEC] + [ANY_SPEC] * 4,
        out_specs=[ANY_SPEC] * 3 + [VMEM_SPEC],
        out_shape=[
            jax.ShapeDtypeStruct((rows, width), half),
            jax.ShapeDtypeStruct((rows, width), half),
            jax.ShapeDtypeStruct((high, width), F32),
            jax.ShapeDtypeStruct((1, width), F32),
        ],
        scratch_shapes=[
            VMEM(blocks.shape, half),
            VMEM((ntiles, BLK, BLK), half),
            VMEM((ntiles + 1, BLK, BLK), half),
            VMEM((ntiles + 1, BLK, BLK), half),
            flat,
            flat,
            VMEM((rows, LANES), F32),
            square,
            VMEM((width, width), half),
            square,
            VMEM((3, nsend * BLK, width), half),
            VMEM((ZQ, 2 * step * BLK, width), half),
            VMEM((nsend * BLK, width), half),
            VMEM((rows, width), F32),
        ]
        + [flat] * 7
        + [
            VMEM((ZQ, 2 * step, BLK, width), half),
            VMEM((nsend, BLK, width), half),
        ]
        + [VMEM((nsend + 1, BLK, width), half)] * 3
        + [VMEM((high, width), F32)]
        + [square] * 3
        + [
            VMEM((8, width), F32),
            VMEM((2 * nbits, 8, width), F32),
            VMEM((high, width), F32),
            VMEM((3 * nblock + 8, LANES), jnp.int32),
            pltpu.SMEM((3 * nblock + 8, LANES), jnp.int32),
            sem((5,)),
            sem((2, ZQ)),
            sem((2, ZQ)),
            sem,
            sem,
            sem,
            sem,
            sem((CQ,)),
            sem((CQ,)),
            sem((CQ,)),
            sem((CQ,)),
            sem((2, ZQ)),
            sem((2, ZQ)),
            sem,
            sem,
        ]
        + [sem((nbits,))] * 6
        + [sem((CQ + 2,))],
        compiler_params=pltpu.CompilerParams(
            vmem_limit_bytes=58 << 20, collective_id=0, has_side_effects=True
        ),
        name="layer",
    )(cols, sends, pins, bias.reshape(1, width), blocks, tiles.reshape(ntiles, BLK, BLK), weight, cotan)


def emit_kernel(count, *refs):
    given, taken, held = refs[:count], refs[count : 2 * count], refs[2 * count : 3 * count]
    sems = refs[-1]
    reads = [pltpu.make_async_copy(given[i], held[i], sems.at[0, i]) for i in range(count)]
    writes = [pltpu.make_async_copy(held[i], taken[i], sems.at[1, i]) for i in range(count)]
    for read in reads:
        read.start()
    for read, write in zip(reads, writes):
        read.wait()
        write.start()
    for write in writes:
        write.wait()


def emit_call(*arrays):
    count = len(arrays)
    return pl.pallas_call(
        functools.partial(emit_kernel, count),
        in_specs=[ANY_SPEC] * count,
        out_specs=[ANY_SPEC] * count,
        out_shape=[jax.ShapeDtypeStruct(one.shape, one.dtype) for one in arrays],
        scratch_shapes=[VMEM(one.shape, one.dtype) for one in arrays]
        + [pltpu.SemaphoreType.DMA((2, count))],
        compiler_params=pltpu.CompilerParams(vmem_limit_bytes=56 << 20),
        name="emit",
    )(*arrays)


def body(feats, tiles, tile_cols, sends, pins, weight, bias, cotan):
    nbits = lax.axis_size("dom").bit_length() - 1
    shifts = (0, nbits // 2, nbits - 1)
    out, dfeat, dweight, dbias = layer_call(
        tile_cols, jnp.transpose(sends, (1, 0, 2)), pins, bias, feats, tiles, weight, cotan, shifts, nbits
    )
    out, dfeat, dweight, dbias = emit_call(out, dfeat, dweight, dbias)
    return (out, dfeat, dweight, dbias.reshape(-1))


def solution(mesh):
    return jax.shard_map(
        body,
        mesh=mesh,
        in_specs=(
            P(("basin", "dom"), "hid"),
            P(("basin", "dom"), None, None, None),
            P(("basin", "dom"), None),
            P(("basin", "dom"), None, None),
            P(("basin", "dom"), None),
            P(None, "hid"),
            P("hid"),
            P(("basin", "dom"), "hid"),
        ),
        out_specs=(
            P(("basin", "dom"), "hid"),
            P(("basin", "dom"), "hid"),
            P("basin", "hid"),
            P(("basin", "hid")),
        ),
        check_vma=False,
    )
```

```python
import functools
import math

import jax
import jax.numpy as jnp
from jax import lax
from jax.experimental import pallas as pl
from jax.experimental.pallas import tpu as pltpu
from jax.sharding import PartitionSpec as P

BLK = 128
LANES = 128
ZQ = 8
CQ = 4
GROUP = 4
VMEM = pltpu.VMEM
F32 = jnp.float32

MESH = pl.DeviceIdType.MESH
SMEM_SPEC = pl.BlockSpec(memory_space=pltpu.SMEM)
VMEM_SPEC = pl.BlockSpec(memory_space=pltpu.VMEM)
ANY_SPEC = pl.BlockSpec(memory_space=pl.ANY)
HBM_SPEC = pl.BlockSpec(memory_space=pltpu.HBM)
FEEDS = (2, 1, 2, 3)

DEEP = (((0,), (0,)), ((), ()))


def flipped(index, bit):
    return index + (1 - 2 * ((index // (1 << bit)) % 2)) * (1 << bit)


def tables(cols, sends_ref):
    nblock, ntile = cols.shape
    nsend = sends_ref.shape[2]
    lane = lax.broadcasted_iota(jnp.int32, (nblock, LANES), 1)
    row = lax.broadcasted_iota(jnp.int32, (nblock, LANES), 0)
    wide = jnp.concatenate([cols, jnp.full((nblock, LANES - ntile), LANES, jnp.int32)], axis=1)
    one = [jnp.broadcast_to(cols[:, k : k + 1], (nblock, LANES)) for k in range(ntile)]
    rank = jnp.zeros((nblock, LANES), jnp.int32)
    upto = jnp.zeros((nblock, LANES), jnp.int32)
    same = jnp.zeros((nblock, LANES), jnp.int32)
    for k in range(ntile):
        before = (one[k] < wide) | ((one[k] == wide) & (k < lane))
        rank = rank + jnp.where(before, 1, 0)
        upto = upto + jnp.where(one[k] <= lane, 1, 0)
        same = same + jnp.where(one[k] == lane, 1, 0)
    merged = jnp.where(same > 0, row * ntile + upto - 1, nblock * ntile)
    perm = jnp.zeros((nblock, LANES), jnp.int32)
    here = jnp.full((nblock, LANES), -1, jnp.int32)
    prev = jnp.full((nblock, LANES), -2, jnp.int32)
    for k in range(ntile):
        at = jnp.broadcast_to(rank[:, k : k + 1], (nblock, LANES))
        perm = perm + jnp.where(at == lane, row * ntile + k, 0)
        here = jnp.where(at == lane, one[k], here)
        prev = jnp.where(at + 1 == lane, one[k], prev)
    chain = jnp.where(here == prev, 1, 0)
    lanes = lax.broadcasted_iota(jnp.int32, (8, LANES), 1)
    rows = lax.broadcasted_iota(jnp.int32, (8, LANES), 0)
    inverse = jnp.full((8, LANES), nsend, jnp.int32)
    for m in range(3):
        for j in range(nsend):
            inverse = jnp.where((lanes == sends_ref[m, 0, j]) & (rows == m), j, inverse)
    return jnp.concatenate([perm, chain, merged, inverse], axis=0)


def layer_kernel(
    shifts, nbits,
    cols_ref, sends_ref, pins_ref, bias_ref, feats_hbm, tiles_hbm, w_hbm, cotan_hbm,
    out_hbm, dfeat_hbm, dw_hbm, db_ref,
    feats, held, fold, turned, cotan, kcot, keep, w, wx, wp, wt,
    outbox, rz, r0, acc, agg, other, dpre, dother, dagg, outv, dfv,
    bz, b0, in0, in1, in2, wsum, outw, inw, gath, bsum, btmp, dwv, tabv, tab,
    fetch_sem, zsend, zrecv, msend, mrecv, xsend, xrecv, asend, arecv, dsend, drecv,
    bsend, brecv, nsend_sem, nrecv_sem, rsend, rrecv, gsend, grecv, vsend, vrecv, put_sem,
):
    nblock, ntile = cols_ref.shape
    width = feats.shape[2]
    rows = nblock * BLK
    ntiles = nblock * ntile
    high = w.shape[0]
    nsend = sends_ref.shape[2]
    step = nsend // ZQ
    merged = 2 * nblock
    inverse = 3 * nblock
    me = lax.axis_index("dom")
    hid = lax.axis_index("hid")
    peer = 1 - hid

    def wide(start, size):
        return pl.ds(pl.multiple_of(start, 16), size)

    here = wide(hid * width, width)
    there = wide(peer * width, width)

    def remote(src, dst, send, recv, where):
        return pltpu.make_async_remote_copy(
            src_ref=src, dst_ref=dst, send_sem=send, recv_sem=recv,
            device_id=where, device_id_type=MESH,
        )

    def mate(bit):
        return {"dom": flipped(me, bit)}

    get_feats = pltpu.make_async_copy(feats_hbm, feats, fetch_sem.at[0])
    get_tiles = pltpu.make_async_copy(tiles_hbm, held, fetch_sem.at[1])
    get_w = pltpu.make_async_copy(w_hbm, w, fetch_sem.at[2])
    get_cotan = pltpu.make_async_copy(cotan_hbm, cotan, fetch_sem.at[3])
    get_feats.start()

    barrier = pltpu.get_barrier_semaphore()
    for bit in range(nbits):
        pl.semaphore_signal(barrier, inc=1, device_id=mate(bit), device_id_type=MESH)
    pl.semaphore_signal(barrier, inc=1, device_id={"hid": peer}, device_id_type=MESH)
    get_w.start()
    get_tiles.start()
    get_cotan.start()

    def zcopy(m, q):
        part = pl.ds((2 - m) * step * BLK, step * BLK)
        return remote(
            outbox.at[m, pl.ds(q * step * BLK, step * BLK)], rz.at[q, part],
            zsend.at[m - 1, q], zrecv.at[m - 1, q], mate(shifts[m]),
        )

    def mcopy():
        return remote(outbox.at[0], r0, msend, mrecv, mate(shifts[0]))

    get_feats.wait()
    for m in (2, 1, 0):
        for j in range(nsend):
            outbox[m, j * BLK : (j + 1) * BLK] = feats[sends_ref[m, 0, j]]
    get_w.wait()
    pl.semaphore_wait(barrier, nbits + 1)
    for q in range(ZQ):
        zcopy(2, q).start()
        zcopy(1, q).start()
        if q == 0:
            mcopy().start()
    wcopy = remote(w.at[there], wx, xsend, xrecv, {"hid": peer})
    wcopy.start()

    tabv[...] = tables(cols_ref[...], sends_ref)
    get_tab = pltpu.make_async_copy(tabv, tab, fetch_sem.at[4])
    get_tab.start()
    fold[ntiles] = jnp.zeros((BLK, BLK), fold.dtype)
    turned[ntiles] = jnp.zeros((BLK, BLK), turned.dtype)
    for ref in (in0, in1, in2):
        ref[nsend] = jnp.zeros((BLK, width), ref.dtype)
    get_tab.wait()
    get_tiles.wait()

    def fold_row(r, carry):
        total = jnp.zeros((BLK, BLK), F32)
        for n in range(ntile):
            link = tab[nblock + r, n].astype(F32)
            total = total * link + held[tab[r, n]].astype(F32)
            value = total.astype(fold.dtype)
            fold[r * ntile + n] = value
            turned[r * ntile + n] = value.T
        return carry

    lax.fori_loop(0, nblock, fold_row, 0)

    def gathered(i, sources):
        return jnp.concatenate(
            [
                jnp.concatenate([fold[tab[merged + i * GROUP + g, s]] for s in sources], axis=1)
                for g in range(GROUP)
            ],
            axis=0,
        )

    def span_of(i):
        return wide(i * GROUP * BLK, GROUP * BLK)

    def own_part(i, carry):
        acc[span_of(i), :] = jnp.dot(
            gathered(i, range(nblock)), feats[...].reshape(rows, width), preferred_element_type=F32
        )
        return carry

    lax.fori_loop(0, nblock // GROUP, own_part, 0)

    get_cotan.wait()
    chunk = 256

    def keep_part(i, carry):
        span = wide(i * chunk, chunk)
        ids = lax.broadcasted_iota(jnp.int32, (chunk, pins_ref.shape[1]), 0) + i * chunk
        hit = jnp.where(ids == pins_ref[...], 1.0, 0.0)
        kept = jnp.broadcast_to(1.0 - jnp.max(hit, axis=1, keepdims=True), (chunk, LANES))
        keep[span, :] = kept
        both = jnp.concatenate([kept] * (width // LANES), axis=1)
        kcot[span, :] = (cotan[span, :].astype(F32) * both).astype(kcot.dtype)
        return carry

    lax.fori_loop(0, rows // chunk, keep_part, 0)
    wp[0:width] = w[here, :]
    wp[width : 2 * width] = w[there, :]
    wt[0:width] = w[here, :].T
    wcopy.wait()
    wt[width : 2 * width] = wx[...].T

    mcopy().wait()

    def near_part(i, carry):
        acc[span_of(i), :] += jnp.dot(
            gathered(i, range(nblock, nblock + nsend)), r0[...], preferred_element_type=F32
        )
        return carry

    lax.fori_loop(0, nblock // GROUP, near_part, 0)

    def far_sources(q):
        return [nblock + m * nsend + q * step + j for m in (2, 1) for j in range(step)]

    def far_part(q, i):
        return acc[span_of(i), :] + jnp.dot(
            gathered(i, far_sources(q)), rz[q], preferred_element_type=F32
        )

    for q in range(ZQ - 1):
        zcopy(2, q).wait()
        zcopy(1, q).wait()

        def some_part(i, carry, q=q):
            acc[span_of(i), :] = far_part(q, i)
            return carry

        lax.fori_loop(0, nblock // GROUP, some_part, 0)

    part = rows // CQ

    def piece(c):
        return wide(c * part, part)

    def acopy(c):
        return remote(
            agg.at[piece(c)], other.at[piece(c)], asend.at[c], arecv.at[c], {"hid": peer}
        )

    def dcopy(c):
        return remote(
            dpre.at[piece(c)], dother.at[piece(c)], dsend.at[c], drecv.at[c], {"hid": peer}
        )

    def ocopy(c):
        return pltpu.make_async_copy(outv.at[piece(c)], out_hbm.at[piece(c)], put_sem.at[c])

    zcopy(2, ZQ - 1).wait()
    zcopy(1, ZQ - 1).wait()

    def last_part(i, carry):
        agg[span_of(i), :] = far_part(ZQ - 1, i).astype(agg.dtype)
        acopy(i).start()
        return carry

    lax.fori_loop(0, nblock // GROUP, last_part, 0)

    def middle(c, carry):
        acopy(c).wait()

        def inner(i, carry):
            span = wide(c * part + i * chunk, chunk)
            full = jnp.concatenate([agg[span, :], other[span, :]], axis=1)
            pre = jnp.dot(full, wp[...], preferred_element_type=F32) + bias_ref[...]
            both = jnp.concatenate([keep[span, :]] * (width // LANES), axis=1)
            sig = jax.nn.sigmoid(pre)
            gate = pre * sig
            at = pl.ds(c * (part // BLK) + i * (chunk // BLK), chunk // BLK)
            old = feats[at].reshape(chunk, width).astype(F32)
            outv[span, :] = (old + both * gate).astype(outv.dtype)
            dpre[span, :] = (
                kcot[span, :].astype(F32) * (sig * (1.0 + pre * (1.0 - sig)))
            ).astype(dpre.dtype)
            return carry

        lax.fori_loop(0, part // chunk, inner, 0)
        dcopy(c).start()
        ocopy(c).start()
        return carry

    lax.fori_loop(0, CQ, middle, 0)

    wsum[...] = jnp.zeros_like(wsum)
    bsum[...] = jnp.zeros_like(bsum)

    def deep(c, carry):
        span = piece(c)
        grad = dpre[span, :]
        full = jnp.concatenate([agg[span, :], other[span, :]], axis=1)
        wsum[...] += lax.dot_general(full, grad, DEEP, preferred_element_type=F32)
        bsum[...] += jnp.sum(grad.astype(F32).reshape(part // 8, 8, width), axis=0)
        return carry

    lax.fori_loop(0, CQ, deep, 0)

    state = {"start": me * 0, "size": high, "at": 0}
    last_bit = nbits - 1

    def sum_start(bit):
        at = state["at"]
        if bit < last_bit:
            half = state["size"] // 2
            upper = (me // (1 << bit)) % 2
            give = state["start"] + (1 - upper) * half
            state["start"] = state["start"] + upper * half
            state["size"] = half
        else:
            half, give = state["size"], state["start"]
        outw[at : at + half] = wsum[wide(give, half)].astype(outw.dtype)
        outgoing = bsum if bit == 0 else btmp.at[2 * bit - 1]
        copies = (
            remote(outw.at[pl.ds(at, half)], inw.at[pl.ds(at, half)], rsend.at[bit], rrecv.at[bit], mate(bit)),
            remote(outgoing, btmp.at[2 * bit], vsend.at[bit], vrecv.at[bit], mate(bit)),
        )
        for copy in copies:
            copy.start()
        return copies

    def sum_end(bit, copies):
        for copy in copies:
            copy.wait()
        half, at = state["size"], state["at"]
        span = wide(state["start"], half)
        came = inw[at : at + half].astype(F32)
        if bit < last_bit:
            wsum[span] += came
        else:
            gath[span] = (outw[at : at + half].astype(F32) + came).astype(gath.dtype)
        outgoing = bsum[...] if bit == 0 else btmp[2 * bit - 1]
        btmp[2 * bit + 1] = outgoing + btmp[2 * bit]
        state["at"] = at + half

    def gather_start(bit):
        span = wide(state["start"], state["size"])
        copy = remote(gath.at[span], gath.at[span], gsend.at[bit], grecv.at[bit], mate(bit))
        copy.start()
        return (copy,)

    def gather_end(bit, copies):
        for copy in copies:
            copy.wait()
        state["start"] = state["start"] - ((me // (1 << bit)) % 2) * state["size"]
        state["size"] = state["size"] * 2

    stages = [(sum_start, sum_end, bit) for bit in range(nbits)]
    stages += [(gather_start, gather_end, bit) for bit in reversed(range(last_bit))]

    flying = stages[0][0](stages[0][2])

    def undo(c, carry):
        dcopy(c).wait()
        span = piece(c)
        both = jnp.concatenate([dpre[span, :], dother[span, :]], axis=1)
        dagg[span, :] = jnp.dot(both, wt[...], preferred_element_type=F32).astype(dagg.dtype)
        return carry

    lax.fori_loop(0, CQ, undo, 0)

    def spread(sources):
        lhs = jnp.concatenate(
            [
                jnp.concatenate([turned[tab[merged + r, s]] for r in range(nblock)], axis=1)
                for s in sources
            ],
            axis=0,
        )
        return jnp.dot(lhs, dagg[...], preferred_element_type=F32)

    boxes = {1: in1, 2: in2}

    def bcopy(m, q):
        return remote(
            bz.at[q, pl.ds((2 - m) * step, step)], boxes[m].at[pl.ds(q * step, step)],
            bsend.at[m - 1, q], brecv.at[m - 1, q], mate(shifts[m]),
        )

    def far_back(q, carry):
        bz[q] = spread(far_sources(q)).astype(bz.dtype).reshape(2 * step, BLK, width)
        bcopy(2, q).start()
        bcopy(1, q).start()
        return carry

    def near_back(i, carry):
        sources = [nblock + i * GROUP + g for g in range(GROUP)]
        b0[pl.ds(i * GROUP, GROUP)] = spread(sources).astype(b0.dtype).reshape(GROUP, BLK, width)
        return carry

    lax.fori_loop(0, nsend // GROUP, near_back, 0)
    ncopy = remote(b0, in0.at[pl.ds(0, nsend)], nsend_sem, nrecv_sem, mate(shifts[0]))

    def own_back(i, carry):
        span = span_of(i)
        acc[span, :] = cotan[span, :].astype(F32) + spread([i * GROUP + g for g in range(GROUP)])
        return carry

    def feed(stage, fed):
        count = FEEDS[stage] if stage < len(FEEDS) else 0
        lax.fori_loop(fed, fed + count, far_back, 0)
        return fed + count

    fed = feed(0, 0)
    lax.fori_loop(0, nsend // GROUP, near_back, 0)
    groups = nblock // GROUP
    for i in range(len(stages)):
        stages[i][1](stages[i][2], flying)
        if i + 1 < len(stages):
            flying = stages[i + 1][0](stages[i + 1][2])
            fed = feed(i + 1, fed)
        if i == 0:
            ncopy.start()
        if i < 2:
            lax.fori_loop(i * groups // 2, (i + 1) * groups // 2, own_back, 0)
        if i == len(stages) - 2:
            ncopy.wait()
    scale = 1.0 / math.sqrt((1 << nbits) * rows)
    dwv[here] = gath[0:width].astype(F32) * scale
    dwv[there] = gath[width : 2 * width].astype(F32) * scale
    put_dw = pltpu.make_async_copy(dwv, dw_hbm, put_sem.at[CQ])
    put_dw.start()
    db_ref[...] = jnp.sum(btmp[2 * nbits - 1], axis=0, keepdims=True) * scale

    for q in range(ZQ):
        bcopy(2, q).wait()
        bcopy(1, q).wait()

    def join(b, carry):
        span = wide(b * BLK, BLK)
        total = acc[span, :]
        for m, ref in enumerate((in0, in1, in2)):
            total = total + ref[tab[inverse + m, b]].astype(F32)
        dfv[span, :] = total.astype(dfv.dtype)
        return carry

    lax.fori_loop(0, nblock, join, 0)
    put_df = pltpu.make_async_copy(dfv, dfeat_hbm, put_sem.at[CQ + 1])
    put_df.start()
    for c in range(CQ):
        ocopy(c).wait()
    put_dw.wait()
    put_df.wait()


def layer_call(cols, sends, pins, bias, feats, tiles, weight, cotan, shifts, nbits):
    rows, width = feats.shape
    nblock, ntile = cols.shape
    ntiles = nblock * ntile
    high = weight.shape[0]
    nsend = sends.shape[2]
    step = nsend // ZQ
    blocks = feats.reshape(nblock, BLK, width)
    sem = pltpu.SemaphoreType.DMA
    half = feats.dtype
    flat = VMEM((rows, width), half)
    square = VMEM((high, width), half)
    return pl.pallas_call(
        functools.partial(layer_kernel, shifts, nbits),
        in_specs=[VMEM_SPEC, SMEM_SPEC, VMEM_SPEC, VMEM_SPEC] + [HBM_SPEC] * 4,
        out_specs=[ANY_SPEC] * 3 + [VMEM_SPEC],
        out_shape=[
            jax.ShapeDtypeStruct((rows, width), half),
            jax.ShapeDtypeStruct((rows, width), half),
            jax.ShapeDtypeStruct((high, width), F32),
            jax.ShapeDtypeStruct((1, width), F32),
        ],
        scratch_shapes=[
            VMEM(blocks.shape, half),
            VMEM((ntiles, BLK, BLK), half),
            VMEM((ntiles + 1, BLK, BLK), half),
            VMEM((ntiles + 1, BLK, BLK), half),
            flat,
            flat,
            VMEM((rows, LANES), F32),
            square,
            VMEM((width, width), half),
            square,
            square,
            VMEM((3, nsend * BLK, width), half),
            VMEM((ZQ, 2 * step * BLK, width), half),
            VMEM((nsend * BLK, width), half),
            VMEM((rows, width), F32),
        ]
        + [flat] * 7
        + [
            VMEM((ZQ, 2 * step, BLK, width), half),
            VMEM((nsend, BLK, width), half),
        ]
        + [VMEM((nsend + 1, BLK, width), half)] * 3
        + [VMEM((high, width), F32)]
        + [square] * 3
        + [
            VMEM((8, width), F32),
            VMEM((2 * nbits, 8, width), F32),
            VMEM((high, width), F32),
            VMEM((3 * nblock + 8, LANES), jnp.int32),
            pltpu.SMEM((3 * nblock + 8, LANES), jnp.int32),
            sem((5,)),
            sem((2, ZQ)),
            sem((2, ZQ)),
            sem,
            sem,
            sem,
            sem,
            sem((CQ,)),
            sem((CQ,)),
            sem((CQ,)),
            sem((CQ,)),
            sem((2, ZQ)),
            sem((2, ZQ)),
            sem,
            sem,
        ]
        + [sem((nbits,))] * 6
        + [sem((CQ + 2,))],
        compiler_params=pltpu.CompilerParams(
            vmem_limit_bytes=58 << 20, collective_id=0, has_side_effects=True
        ),
        name="layer",
    )(cols, sends, pins, bias.reshape(1, width), blocks, tiles.reshape(ntiles, BLK, BLK), weight, cotan)


def emit_kernel(count, *refs):
    given, taken, held = refs[:count], refs[count : 2 * count], refs[2 * count : 3 * count]
    sems = refs[-1]
    reads = [pltpu.make_async_copy(given[i], held[i], sems.at[0, i]) for i in range(count)]
    writes = [pltpu.make_async_copy(held[i], taken[i], sems.at[1, i]) for i in range(count)]
    for read in reads:
        read.start()
    for read, write in zip(reads, writes):
        read.wait()
        write.start()
    for write in writes:
        write.wait()


def emit_call(*arrays):
    count = len(arrays)
    return pl.pallas_call(
        functools.partial(emit_kernel, count),
        in_specs=[ANY_SPEC] * count,
        out_specs=[ANY_SPEC] * count,
        out_shape=[jax.ShapeDtypeStruct(one.shape, one.dtype) for one in arrays],
        scratch_shapes=[VMEM(one.shape, one.dtype) for one in arrays]
        + [pltpu.SemaphoreType.DMA((2, count))],
        compiler_params=pltpu.CompilerParams(vmem_limit_bytes=56 << 20),
        name="emit",
    )(*arrays)


def body(feats, tiles, tile_cols, sends, pins, weight, bias, cotan):
    nbits = lax.axis_size("dom").bit_length() - 1
    shifts = (0, nbits // 2, nbits - 1)
    out, dfeat, dweight, dbias = layer_call(
        tile_cols, jnp.transpose(sends, (1, 0, 2)), pins, bias, feats, tiles, weight, cotan, shifts, nbits
    )
    out, dfeat, dweight, dbias = emit_call(out, dfeat, dweight, dbias)
    return (out, dfeat, dweight, dbias.reshape(-1))


def solution(mesh):
    return jax.shard_map(
        body,
        mesh=mesh,
        in_specs=(
            P(("basin", "dom"), "hid"),
            P(("basin", "dom"), None, None, None),
            P(("basin", "dom"), None),
            P(("basin", "dom"), None, None),
            P(("basin", "dom"), None),
            P(None, "hid"),
            P("hid"),
            P(("basin", "dom"), "hid"),
        ),
        out_specs=(
            P(("basin", "dom"), "hid"),
            P(("basin", "dom"), "hid"),
            P("basin", "hid"),
            P(("basin", "hid")),
        ),
        check_vma=False,
    )
```

```python
import functools
import math

import jax
import jax.numpy as jnp
from jax import lax
from jax.experimental import pallas as pl
from jax.experimental.pallas import tpu as pltpu
from jax.sharding import PartitionSpec as P

BLK = 128
LANES = 128
ZQ = 8
CQ = 4
GROUP = 4
VMEM = pltpu.VMEM
F32 = jnp.float32

MESH = pl.DeviceIdType.MESH
SMEM_SPEC = pl.BlockSpec(memory_space=pltpu.SMEM)
VMEM_SPEC = pl.BlockSpec(memory_space=pltpu.VMEM)
ANY_SPEC = pl.BlockSpec(memory_space=pl.ANY)
HBM_SPEC = pl.BlockSpec(memory_space=pltpu.HBM)
FEEDS = (2, 1, 2, 3)

DEEP = (((0,), (0,)), ((), ()))


def flipped(index, bit):
    return index + (1 - 2 * ((index // (1 << bit)) % 2)) * (1 << bit)


def tables(cols):
    nblock, ntile = cols.shape
    lane = lax.broadcasted_iota(jnp.int32, (nblock, LANES), 1)
    row = lax.broadcasted_iota(jnp.int32, (nblock, LANES), 0)
    wide = jnp.concatenate([cols, jnp.full((nblock, LANES - ntile), LANES, jnp.int32)], axis=1)
    one = [jnp.broadcast_to(cols[:, k : k + 1], (nblock, LANES)) for k in range(ntile)]
    rank = jnp.zeros((nblock, LANES), jnp.int32)
    upto = jnp.zeros((nblock, LANES), jnp.int32)
    same = jnp.zeros((nblock, LANES), jnp.int32)
    for k in range(ntile):
        before = (one[k] < wide) | ((one[k] == wide) & (k < lane))
        rank = rank + jnp.where(before, 1, 0)
        upto = upto + jnp.where(one[k] <= lane, 1, 0)
        same = same + jnp.where(one[k] == lane, 1, 0)
    merged = jnp.where(same > 0, row * ntile + upto - 1, nblock * ntile)
    perm = jnp.zeros((nblock, LANES), jnp.int32)
    here = jnp.full((nblock, LANES), -1, jnp.int32)
    prev = jnp.full((nblock, LANES), -2, jnp.int32)
    for k in range(ntile):
        at = jnp.broadcast_to(rank[:, k : k + 1], (nblock, LANES))
        perm = perm + jnp.where(at == lane, row * ntile + k, 0)
        here = jnp.where(at == lane, one[k], here)
        prev = jnp.where(at + 1 == lane, one[k], prev)
    chain = jnp.where(here == prev, 1, 0)
    return jnp.concatenate([perm, chain, merged], axis=0)


def layer_kernel(
    shifts, nbits,
    cols_ref, sends_ref, pins_ref, bias_ref, feats_hbm, tiles_hbm, w_hbm, cotan_hbm,
    outv, acc, in0, in1, in2, dwv, db_ref,
    feats, held, fold, turned, cotan, kcot, keep, w, wx, wp, wt,
    outbox, rz, r0, agg, other, dpre, dother, dagg,
    bz, b0, wsum, outw, inw, gath, bsum, btmp, tabv, tab,
    fetch_sem, zsend, zrecv, msend, mrecv, xsend, xrecv, asend, arecv, dsend, drecv,
    bsend, brecv, nsend_sem, nrecv_sem, rsend, rrecv, gsend, grecv, vsend, vrecv,
):
    nblock, ntile = cols_ref.shape
    width = feats.shape[2]
    rows = nblock * BLK
    ntiles = nblock * ntile
    high = w.shape[0]
    nsend = sends_ref.shape[2]
    step = nsend // ZQ
    merged = 2 * nblock
    me = lax.axis_index("dom")
    hid = lax.axis_index("hid")
    peer = 1 - hid

    def wide(start, size):
        return pl.ds(pl.multiple_of(start, 16), size)

    here = wide(hid * width, width)
    there = wide(peer * width, width)

    def remote(src, dst, send, recv, where):
        return pltpu.make_async_remote_copy(
            src_ref=src, dst_ref=dst, send_sem=send, recv_sem=recv,
            device_id=where, device_id_type=MESH,
        )

    def mate(bit):
        return {"dom": flipped(me, bit)}

    get_feats = pltpu.make_async_copy(feats_hbm, feats, fetch_sem.at[0])
    get_tiles = pltpu.make_async_copy(tiles_hbm, held, fetch_sem.at[1])
    get_w = pltpu.make_async_copy(w_hbm, w, fetch_sem.at[2])
    get_cotan = pltpu.make_async_copy(cotan_hbm, cotan, fetch_sem.at[3])
    get_feats.start()

    barrier = pltpu.get_barrier_semaphore()
    for bit in range(nbits):
        pl.semaphore_signal(barrier, inc=1, device_id=mate(bit), device_id_type=MESH)
    pl.semaphore_signal(barrier, inc=1, device_id={"hid": peer}, device_id_type=MESH)
    get_w.start()
    get_tiles.start()
    get_cotan.start()

    def zcopy(m, q):
        part = pl.ds((2 - m) * step * BLK, step * BLK)
        return remote(
            outbox.at[m, pl.ds(q * step * BLK, step * BLK)], rz.at[q, part],
            zsend.at[m - 1, q], zrecv.at[m - 1, q], mate(shifts[m]),
        )

    def mcopy():
        return remote(outbox.at[0], r0, msend, mrecv, mate(shifts[0]))

    get_feats.wait()
    for m in (2, 1, 0):
        for j in range(nsend):
            outbox[m, j * BLK : (j + 1) * BLK] = feats[sends_ref[m, 0, j]]
    get_w.wait()
    pl.semaphore_wait(barrier, nbits + 1)
    for q in range(ZQ):
        zcopy(2, q).start()
        zcopy(1, q).start()
        if q == 0:
            mcopy().start()
    wcopy = remote(w.at[there], wx, xsend, xrecv, {"hid": peer})
    wcopy.start()

    tabv[...] = tables(cols_ref[...])
    get_tab = pltpu.make_async_copy(tabv, tab, fetch_sem.at[4])
    get_tab.start()
    fold[ntiles] = jnp.zeros((BLK, BLK), fold.dtype)
    turned[ntiles] = jnp.zeros((BLK, BLK), turned.dtype)
    get_tab.wait()
    get_tiles.wait()

    def fold_row(r, carry):
        total = jnp.zeros((BLK, BLK), F32)
        for n in range(ntile):
            link = tab[nblock + r, n].astype(F32)
            total = total * link + held[tab[r, n]].astype(F32)
            value = total.astype(fold.dtype)
            fold[r * ntile + n] = value
            turned[r * ntile + n] = value.T
        return carry

    lax.fori_loop(0, nblock, fold_row, 0)

    def gathered(i, sources):
        return jnp.concatenate(
            [
                jnp.concatenate([fold[tab[merged + i * GROUP + g, s]] for s in sources], axis=1)
                for g in range(GROUP)
            ],
            axis=0,
        )

    def span_of(i):
        return wide(i * GROUP * BLK, GROUP * BLK)

    def own_part(i, carry):
        acc[span_of(i), :] = jnp.dot(
            gathered(i, range(nblock)), feats[...].reshape(rows, width), preferred_element_type=F32
        )
        return carry

    lax.fori_loop(0, nblock // GROUP, own_part, 0)

    get_cotan.wait()
    chunk = 256

    def keep_part(i, carry):
        span = wide(i * chunk, chunk)
        ids = lax.broadcasted_iota(jnp.int32, (chunk, pins_ref.shape[1]), 0) + i * chunk
        hit = jnp.where(ids == pins_ref[...], 1.0, 0.0)
        kept = jnp.broadcast_to(1.0 - jnp.max(hit, axis=1, keepdims=True), (chunk, LANES))
        keep[span, :] = kept
        both = jnp.concatenate([kept] * (width // LANES), axis=1)
        kcot[span, :] = (cotan[span, :].astype(F32) * both).astype(kcot.dtype)
        return carry

    lax.fori_loop(0, rows // chunk, keep_part, 0)
    wp[0:width] = w[here, :]
    wp[width : 2 * width] = w[there, :]
    wt[0:width] = w[here, :].T
    wcopy.wait()
    wt[width : 2 * width] = wx[...].T

    mcopy().wait()

    def near_part(i, carry):
        acc[span_of(i), :] += jnp.dot(
            gathered(i, range(nblock, nblock + nsend)), r0[...], preferred_element_type=F32
        )
        return carry

    lax.fori_loop(0, nblock // GROUP, near_part, 0)

    def far_sources(q):
        return [nblock + m * nsend + q * step + j for m in (2, 1) for j in range(step)]

    def far_part(q, i):
        return acc[span_of(i), :] + jnp.dot(
            gathered(i, far_sources(q)), rz[q], preferred_element_type=F32
        )

    for q in range(ZQ - 1):
        zcopy(2, q).wait()
        zcopy(1, q).wait()

        def some_part(i, carry, q=q):
            acc[span_of(i), :] = far_part(q, i)
            return carry

        lax.fori_loop(0, nblock // GROUP, some_part, 0)

    part = rows // CQ

    def piece(c):
        return wide(c * part, part)

    def acopy(c):
        return remote(
            agg.at[piece(c)], other.at[piece(c)], asend.at[c], arecv.at[c], {"hid": peer}
        )

    def dcopy(c):
        return remote(
            dpre.at[piece(c)], dother.at[piece(c)], dsend.at[c], drecv.at[c], {"hid": peer}
        )

    zcopy(2, ZQ - 1).wait()
    zcopy(1, ZQ - 1).wait()

    def last_part(i, carry):
        agg[span_of(i), :] = far_part(ZQ - 1, i).astype(agg.dtype)
        acopy(i).start()
        return carry

    lax.fori_loop(0, nblock // GROUP, last_part, 0)

    def middle(c, carry):
        acopy(c).wait()

        def inner(i, carry):
            span = wide(c * part + i * chunk, chunk)
            full = jnp.concatenate([agg[span, :], other[span, :]], axis=1)
            pre = jnp.dot(full, wp[...], preferred_element_type=F32) + bias_ref[...]
            both = jnp.concatenate([keep[span, :]] * (width // LANES), axis=1)
            sig = jax.nn.sigmoid(pre)
            gate = pre * sig
            at = pl.ds(c * (part // BLK) + i * (chunk // BLK), chunk // BLK)
            old = feats[at].reshape(chunk, width).astype(F32)
            outv[span, :] = (old + both * gate).astype(outv.dtype)
            dpre[span, :] = (
                kcot[span, :].astype(F32) * (sig * (1.0 + pre * (1.0 - sig)))
            ).astype(dpre.dtype)
            return carry

        lax.fori_loop(0, part // chunk, inner, 0)
        dcopy(c).start()
        return carry

    lax.fori_loop(0, CQ, middle, 0)

    wsum[...] = jnp.zeros_like(wsum)
    bsum[...] = jnp.zeros_like(bsum)

    def deep(c, carry):
        span = piece(c)
        grad = dpre[span, :]
        full = jnp.concatenate([agg[span, :], other[span, :]], axis=1)
        wsum[...] += lax.dot_general(full, grad, DEEP, preferred_element_type=F32)
        bsum[...] += jnp.sum(grad.astype(F32).reshape(part // 8, 8, width), axis=0)
        return carry

    lax.fori_loop(0, CQ, deep, 0)

    state = {"start": me * 0, "size": high, "at": 0}
    last_bit = nbits - 1

    def sum_start(bit):
        at = state["at"]
        if bit < last_bit:
            half = state["size"] // 2
            upper = (me // (1 << bit)) % 2
            give = state["start"] + (1 - upper) * half
            state["start"] = state["start"] + upper * half
            state["size"] = half
        else:
            half, give = state["size"], state["start"]
        outw[at : at + half] = wsum[wide(give, half)].astype(outw.dtype)
        outgoing = bsum if bit == 0 else btmp.at[2 * bit - 1]
        copies = (
            remote(outw.at[pl.ds(at, half)], inw.at[pl.ds(at, half)], rsend.at[bit], rrecv.at[bit], mate(bit)),
            remote(outgoing, btmp.at[2 * bit], vsend.at[bit], vrecv.at[bit], mate(bit)),
        )
        for copy in copies:
            copy.start()
        return copies

    def sum_end(bit, copies):
        for copy in copies:
            copy.wait()
        half, at = state["size"], state["at"]
        span = wide(state["start"], half)
        came = inw[at : at + half].astype(F32)
        if bit < last_bit:
            wsum[span] += came
        else:
            gath[span] = (outw[at : at + half].astype(F32) + came).astype(gath.dtype)
        outgoing = bsum[...] if bit == 0 else btmp[2 * bit - 1]
        btmp[2 * bit + 1] = outgoing + btmp[2 * bit]
        state["at"] = at + half

    def gather_start(bit):
        span = wide(state["start"], state["size"])
        copy = remote(gath.at[span], gath.at[span], gsend.at[bit], grecv.at[bit], mate(bit))
        copy.start()
        return (copy,)

    def gather_end(bit, copies):
        for copy in copies:
            copy.wait()
        state["start"] = state["start"] - ((me // (1 << bit)) % 2) * state["size"]
        state["size"] = state["size"] * 2

    stages = [(sum_start, sum_end, bit) for bit in range(nbits)]
    stages += [(gather_start, gather_end, bit) for bit in reversed(range(last_bit))]

    flying = stages[0][0](stages[0][2])

    def undo(c, carry):
        dcopy(c).wait()
        span = piece(c)
        both = jnp.concatenate([dpre[span, :], dother[span, :]], axis=1)
        dagg[span, :] = jnp.dot(both, wt[...], preferred_element_type=F32).astype(dagg.dtype)
        return carry

    lax.fori_loop(0, CQ, undo, 0)

    def spread(sources):
        lhs = jnp.concatenate(
            [
                jnp.concatenate([turned[tab[merged + r, s]] for r in range(nblock)], axis=1)
                for s in sources
            ],
            axis=0,
        )
        return jnp.dot(lhs, dagg[...], preferred_element_type=F32)

    boxes = {1: in1, 2: in2}

    def bcopy(m, q):
        return remote(
            bz.at[q, pl.ds((2 - m) * step, step)], boxes[m].at[pl.ds(q * step, step)],
            bsend.at[m - 1, q], brecv.at[m - 1, q], mate(shifts[m]),
        )

    def far_back(q, carry):
        bz[q] = spread(far_sources(q)).astype(bz.dtype).reshape(2 * step, BLK, width)
        bcopy(2, q).start()
        bcopy(1, q).start()
        return carry

    def near_back(i, carry):
        sources = [nblock + i * GROUP + g for g in range(GROUP)]
        b0[pl.ds(i * GROUP, GROUP)] = spread(sources).astype(b0.dtype).reshape(GROUP, BLK, width)
        return carry

    lax.fori_loop(0, nsend // GROUP, near_back, 0)
    ncopy = remote(b0, in0, nsend_sem, nrecv_sem, mate(shifts[0]))

    def own_back(i, carry):
        span = span_of(i)
        acc[span, :] = cotan[span, :].astype(F32) + spread([i * GROUP + g for g in range(GROUP)])
        return carry

    def feed(stage, fed):
        count = FEEDS[stage] if stage < len(FEEDS) else 0
        lax.fori_loop(fed, fed + count, far_back, 0)
        return fed + count

    fed = feed(0, 0)
    lax.fori_loop(0, nsend // GROUP, near_back, 0)
    groups = nblock // GROUP
    for i in range(len(stages)):
        stages[i][1](stages[i][2], flying)
        if i + 1 < len(stages):
            flying = stages[i + 1][0](stages[i + 1][2])
            fed = feed(i + 1, fed)
        if i == 0:
            ncopy.start()
        if i < 2:
            lax.fori_loop(i * groups // 2, (i + 1) * groups // 2, own_back, 0)
        if i == len(stages) - 2:
            ncopy.wait()
    scale = 1.0 / math.sqrt((1 << nbits) * rows)
    dwv[here] = gath[0:width].astype(F32) * scale
    dwv[there] = gath[width : 2 * width].astype(F32) * scale
    db_ref[...] = jnp.sum(btmp[2 * nbits - 1], axis=0, keepdims=True) * scale

    for q in range(ZQ):
        bcopy(2, q).wait()
        bcopy(1, q).wait()


def layer_call(cols, sends, pins, bias, feats, tiles, weight, cotan, shifts, nbits):
    rows, width = feats.shape
    nblock, ntile = cols.shape
    ntiles = nblock * ntile
    high = weight.shape[0]
    nsend = sends.shape[2]
    step = nsend // ZQ
    blocks = feats.reshape(nblock, BLK, width)
    sem = pltpu.SemaphoreType.DMA
    half = feats.dtype
    flat = VMEM((rows, width), half)
    square = VMEM((high, width), half)
    return pl.pallas_call(
        functools.partial(layer_kernel, shifts, nbits),
        in_specs=[VMEM_SPEC, SMEM_SPEC, VMEM_SPEC, VMEM_SPEC] + [HBM_SPEC] * 4,
        out_specs=[VMEM_SPEC] * 7,
        out_shape=[flat, VMEM((rows, width), F32)]
        + [VMEM((nsend, BLK, width), half)] * 3
        + [VMEM((high, width), F32), VMEM((1, width), F32)],
        scratch_shapes=[
            VMEM(blocks.shape, half),
            VMEM((ntiles, BLK, BLK), half),
            VMEM((ntiles + 1, BLK, BLK), half),
            VMEM((ntiles + 1, BLK, BLK), half),
            flat,
            flat,
            VMEM((rows, LANES), F32),
            square,
            VMEM((width, width), half),
            square,
            square,
            VMEM((3, nsend * BLK, width), half),
            VMEM((ZQ, 2 * step * BLK, width), half),
            VMEM((nsend * BLK, width), half),
        ]
        + [flat] * 5
        + [
            VMEM((ZQ, 2 * step, BLK, width), half),
            VMEM((nsend, BLK, width), half),
        ]
        + [VMEM((high, width), F32)]
        + [square] * 3
        + [
            VMEM((8, width), F32),
            VMEM((2 * nbits, 8, width), F32),
            VMEM((3 * nblock, LANES), jnp.int32),
            pltpu.SMEM((3 * nblock, LANES), jnp.int32),
            sem((5,)),
            sem((2, ZQ)),
            sem((2, ZQ)),
            sem,
            sem,
            sem,
            sem,
            sem((CQ,)),
            sem((CQ,)),
            sem((CQ,)),
            sem((CQ,)),
            sem((2, ZQ)),
            sem((2, ZQ)),
            sem,
            sem,
        ]
        + [sem((nbits,))] * 6,
        compiler_params=pltpu.CompilerParams(
            vmem_limit_bytes=52 << 20, collective_id=0, has_side_effects=True
        ),
        name="layer",
    )(cols, sends, pins, bias.reshape(1, width), blocks, tiles.reshape(ntiles, BLK, BLK), weight, cotan)


def join_kernel(sends_ref, out_ref, acc_ref, in0_ref, in1_ref, in2_ref, dw_ref, db_ref, out, dfeat, dw, db, lines, inverse, sems):
    nblock = lines.shape[0]
    nsend, _, width = in0_ref.shape
    copies = [
        pltpu.make_async_copy(out_ref, out, sems.at[0]),
        pltpu.make_async_copy(dw_ref, dw, sems.at[1]),
        pltpu.make_async_copy(db_ref, db, sems.at[2]),
    ]
    for copy in copies:
        copy.start()
    for m in range(3):
        for b in range(nblock):
            inverse[m, b] = nsend
        for j in range(nsend):
            inverse[m, sends_ref[m, 0, j]] = j

    def one_block(b, carry):
        span = pl.ds(pl.multiple_of(b * BLK, BLK), BLK)
        total = acc_ref[span, :]
        for m, ref in enumerate((in0_ref, in1_ref, in2_ref)):
            at = inverse[m, b]
            held = ref[jnp.minimum(at, nsend - 1)].astype(F32)
            total = total + held * jnp.where(at < nsend, 1.0, 0.0)
        lines[b] = total.astype(lines.dtype)
        pltpu.make_async_copy(lines.at[b], dfeat.at[b], sems.at[3 + b]).start()
        return carry

    lax.fori_loop(0, nblock, one_block, 0)
    for b in range(nblock):
        pltpu.make_async_copy(lines.at[b], dfeat.at[b], sems.at[3 + b]).wait()
    for copy in copies:
        copy.wait()


def join_call(sends, out, acc, in0, in1, in2, dw, db):
    rows, width = out.shape
    blocks = (rows // BLK, BLK, width)
    return pl.pallas_call(
        join_kernel,
        in_specs=[SMEM_SPEC] + [VMEM_SPEC] * 7,
        out_specs=[HBM_SPEC] * 4,
        out_shape=[
            jax.ShapeDtypeStruct(out.shape, out.dtype),
            jax.ShapeDtypeStruct(blocks, out.dtype),
            jax.ShapeDtypeStruct(dw.shape, dw.dtype),
            jax.ShapeDtypeStruct(db.shape, db.dtype),
        ],
        scratch_shapes=[
            VMEM(blocks, out.dtype),
            pltpu.SMEM((3, blocks[0]), jnp.int32),
            pltpu.SemaphoreType.DMA((3 + blocks[0],)),
        ],
        compiler_params=pltpu.CompilerParams(vmem_limit_bytes=8 << 20),
        name="join",
    )(sends, out, acc, in0, in1, in2, dw, db)


def body(feats, tiles, tile_cols, sends, pins, weight, bias, cotan):
    nbits = lax.axis_size("dom").bit_length() - 1
    shifts = (0, nbits // 2, nbits - 1)
    sends = jnp.transpose(sends, (1, 0, 2))
    results = layer_call(
        tile_cols, sends, pins, bias, feats, tiles, weight, cotan, shifts, nbits
    )
    out, dfeat, dweight, dbias = join_call(sends, *results)
    return (out, dfeat.reshape(feats.shape), dweight, dbias.reshape(-1))


def solution(mesh):
    return jax.shard_map(
        body,
        mesh=mesh,
        in_specs=(
            P(("basin", "dom"), "hid"),
            P(("basin", "dom"), None, None, None),
            P(("basin", "dom"), None),
            P(("basin", "dom"), None, None),
            P(("basin", "dom"), None),
            P(None, "hid"),
            P("hid"),
            P(("basin", "dom"), "hid"),
        ),
        out_specs=(
            P(("basin", "dom"), "hid"),
            P(("basin", "dom"), "hid"),
            P("basin", "hid"),
            P(("basin", "hid")),
        ),
        check_vma=False,
    )
```

```python
import functools
import math

import jax
import jax.numpy as jnp
from jax import lax
from jax.experimental import pallas as pl
from jax.experimental.pallas import tpu as pltpu
from jax.sharding import PartitionSpec as P

BLK = 128
LANES = 128
ZQ = 8
CQ = 4
GROUP = 4
VMEM = pltpu.VMEM
F32 = jnp.float32

MESH = pl.DeviceIdType.MESH
SMEM_SPEC = pl.BlockSpec(memory_space=pltpu.SMEM)
VMEM_SPEC = pl.BlockSpec(memory_space=pltpu.VMEM)
ANY_SPEC = pl.BlockSpec(memory_space=pl.ANY)
HBM_SPEC = pl.BlockSpec(memory_space=pltpu.HBM)
FEEDS = (1, 2, 2, 3)

DEEP = (((0,), (0,)), ((), ()))


def flipped(index, bit):
    return index + (1 - 2 * ((index // (1 << bit)) % 2)) * (1 << bit)


def tables(cols):
    nblock, ntile = cols.shape
    lane = lax.broadcasted_iota(jnp.int32, (nblock, LANES), 1)
    row = lax.broadcasted_iota(jnp.int32, (nblock, LANES), 0)
    wide = jnp.concatenate([cols, jnp.full((nblock, LANES - ntile), LANES, jnp.int32)], axis=1)
    one = [jnp.broadcast_to(cols[:, k : k + 1], (nblock, LANES)) for k in range(ntile)]
    rank = jnp.zeros((nblock, LANES), jnp.int32)
    upto = jnp.zeros((nblock, LANES), jnp.int32)
    same = jnp.zeros((nblock, LANES), jnp.int32)
    for k in range(ntile):
        before = (one[k] < wide) | ((one[k] == wide) & (k < lane))
        rank = rank + jnp.where(before, 1, 0)
        upto = upto + jnp.where(one[k] <= lane, 1, 0)
        same = same + jnp.where(one[k] == lane, 1, 0)
    merged = jnp.where(same > 0, row * ntile + upto - 1, nblock * ntile)
    perm = jnp.zeros((nblock, LANES), jnp.int32)
    here = jnp.full((nblock, LANES), -1, jnp.int32)
    prev = jnp.full((nblock, LANES), -2, jnp.int32)
    for k in range(ntile):
        at = jnp.broadcast_to(rank[:, k : k + 1], (nblock, LANES))
        perm = perm + jnp.where(at == lane, row * ntile + k, 0)
        here = jnp.where(at == lane, one[k], here)
        prev = jnp.where(at + 1 == lane, one[k], prev)
    chain = jnp.where(here == prev, 1, 0)
    return jnp.concatenate([perm, chain, merged], axis=0)


def layer_kernel(
    shifts, nbits,
    cols_ref, sends_ref, pins_ref, bias_ref, feats_hbm, tiles_hbm, w_hbm, cotan_hbm,
    outv, acc, in0, in1, in2, dwv, db_ref,
    feats, held, fold, turned, cotan, kcot, keep, w, wx, wp, wt,
    outbox, rz, r0, agg, other, dpre, dother, dagg,
    bz, b0, wsum, outw, inw, gath, bsum, btmp, tabv, tab,
    fetch_sem, zsend, zrecv, msend, mrecv, xsend, xrecv, asend, arecv, dsend, drecv,
    bsend, brecv, nsend_sem, nrecv_sem, rsend, rrecv, gsend, grecv, vsend, vrecv,
):
    nblock, ntile = cols_ref.shape
    width = feats.shape[2]
    rows = nblock * BLK
    ntiles = nblock * ntile
    high = w.shape[0]
    nsend = sends_ref.shape[2]
    step = nsend // ZQ
    merged = 2 * nblock
    me = lax.axis_index("dom")
    hid = lax.axis_index("hid")
    peer = 1 - hid

    def wide(start, size):
        return pl.ds(pl.multiple_of(start, 16), size)

    here = wide(hid * width, width)
    there = wide(peer * width, width)

    def remote(src, dst, send, recv, where):
        return pltpu.make_async_remote_copy(
            src_ref=src, dst_ref=dst, send_sem=send, recv_sem=recv,
            device_id=where, device_id_type=MESH,
        )

    def mate(bit):
        return {"dom": flipped(me, bit)}

    get_feats = pltpu.make_async_copy(feats_hbm, feats, fetch_sem.at[0])
    get_tiles = pltpu.make_async_copy(tiles_hbm, held, fetch_sem.at[1])
    get_w = pltpu.make_async_copy(w_hbm, w, fetch_sem.at[2])
    get_cotan = pltpu.make_async_copy(cotan_hbm, cotan, fetch_sem.at[3])
    get_feats.start()

    barrier = pltpu.get_barrier_semaphore()
    for bit in range(nbits):
        pl.semaphore_signal(barrier, inc=1, device_id=mate(bit), device_id_type=MESH)
    pl.semaphore_signal(barrier, inc=1, device_id={"hid": peer}, device_id_type=MESH)
    get_w.start()
    get_tiles.start()
    get_cotan.start()

    def zcopy(m, q):
        part = pl.ds((2 - m) * step * BLK, step * BLK)
        return remote(
            outbox.at[m, pl.ds(q * step * BLK, step * BLK)], rz.at[q, part],
            zsend.at[m - 1, q], zrecv.at[m - 1, q], mate(shifts[m]),
        )

    def mcopy():
        return remote(outbox.at[0], r0, msend, mrecv, mate(shifts[0]))

    get_feats.wait()
    for m in (2, 1, 0):
        for j in range(nsend):
            outbox[m, j * BLK : (j + 1) * BLK] = feats[sends_ref[m, 0, j]]
    get_w.wait()
    pl.semaphore_wait(barrier, nbits + 1)
    for q in range(ZQ):
        zcopy(2, q).start()
        zcopy(1, q).start()
        if q == 0:
            mcopy().start()
    wcopy = remote(w.at[there], wx, xsend, xrecv, {"hid": peer})
    wcopy.start()

    tabv[...] = tables(cols_ref[...])
    get_tab = pltpu.make_async_copy(tabv, tab, fetch_sem.at[4])
    get_tab.start()
    fold[ntiles] = jnp.zeros((BLK, BLK), fold.dtype)
    turned[ntiles] = jnp.zeros((BLK, BLK), turned.dtype)
    get_tab.wait()
    get_tiles.wait()

    def fold_row(r, carry):
        total = jnp.zeros((BLK, BLK), F32)
        for n in range(ntile):
            link = tab[nblock + r, n].astype(F32)
            total = total * link + held[tab[r, n]].astype(F32)
            value = total.astype(fold.dtype)
            fold[r * ntile + n] = value
            turned[r * ntile + n] = value.T
        return carry

    lax.fori_loop(0, nblock, fold_row, 0)

    def gathered(i, sources):
        return jnp.concatenate(
            [
                jnp.concatenate([fold[tab[merged + i * GROUP + g, s]] for s in sources], axis=1)
                for g in range(GROUP)
            ],
            axis=0,
        )

    def span_of(i):
        return wide(i * GROUP * BLK, GROUP * BLK)

    def own_part(i, carry):
        acc[span_of(i), :] = jnp.dot(
            gathered(i, range(nblock)), feats[...].reshape(rows, width), preferred_element_type=F32
        )
        return carry

    lax.fori_loop(0, nblock // GROUP, own_part, 0)

    get_cotan.wait()
    chunk = 512

    def keep_part(i, carry):
        span = wide(i * chunk, chunk)
        ids = lax.broadcasted_iota(jnp.int32, (chunk, pins_ref.shape[1]), 0) + i * chunk
        hit = jnp.where(ids == pins_ref[...], 1.0, 0.0)
        kept = jnp.broadcast_to(1.0 - jnp.max(hit, axis=1, keepdims=True), (chunk, LANES))
        keep[span, :] = kept
        both = jnp.concatenate([kept] * (width // LANES), axis=1)
        kcot[span, :] = (cotan[span, :].astype(F32) * both).astype(kcot.dtype)
        return carry

    lax.fori_loop(0, rows // chunk, keep_part, 0)
    wp[0:width] = w[here, :]
    wp[width : 2 * width] = w[there, :]
    wt[0:width] = w[here, :].T
    wcopy.wait()
    wt[width : 2 * width] = wx[...].T

    mcopy().wait()

    def near_part(i, carry):
        acc[span_of(i), :] += jnp.dot(
            gathered(i, range(nblock, nblock + nsend)), r0[...], preferred_element_type=F32
        )
        return carry

    lax.fori_loop(0, nblock // GROUP, near_part, 0)

    def far_sources(q):
        return [nblock + m * nsend + q * step + j for m in (2, 1) for j in range(step)]

    def far_part(q, i):
        return acc[span_of(i), :] + jnp.dot(
            gathered(i, far_sources(q)), rz[q], preferred_element_type=F32
        )

    for q in range(ZQ - 1):
        zcopy(2, q).wait()
        zcopy(1, q).wait()

        def some_part(i, carry, q=q):
            acc[span_of(i), :] = far_part(q, i)
            return carry

        lax.fori_loop(0, nblock // GROUP, some_part, 0)

    part = rows // CQ

    def piece(c):
        return wide(c * part, part)

    def acopy(c):
        return remote(
            agg.at[piece(c)], other.at[piece(c)], asend.at[c], arecv.at[c], {"hid": peer}
        )

    def dcopy(c):
        return remote(
            dpre.at[piece(c)], dother.at[piece(c)], dsend.at[c], drecv.at[c], {"hid": peer}
        )

    zcopy(2, ZQ - 1).wait()
    zcopy(1, ZQ - 1).wait()

    def last_part(i, carry):
        agg[span_of(i), :] = far_part(ZQ - 1, i).astype(agg.dtype)
        acopy(i).start()
        return carry

    lax.fori_loop(0, nblock // GROUP, last_part, 0)

    def middle(c, carry):
        acopy(c).wait()

        def inner(i, carry):
            span = wide(c * part + i * chunk, chunk)
            full = jnp.concatenate([agg[span, :], other[span, :]], axis=1)
            pre = jnp.dot(full, wp[...], preferred_element_type=F32) + bias_ref[...]
            both = jnp.concatenate([keep[span, :]] * (width // LANES), axis=1)
            sig = jax.nn.sigmoid(pre)
            gate = pre * sig
            at = pl.ds(c * (part // BLK) + i * (chunk // BLK), chunk // BLK)
            old = feats[at].reshape(chunk, width).astype(F32)
            outv[span, :] = (old + both * gate).astype(outv.dtype)
            dpre[span, :] = (
                kcot[span, :].astype(F32) * (sig * (1.0 + pre * (1.0 - sig)))
            ).astype(dpre.dtype)
            return carry

        lax.fori_loop(0, part // chunk, inner, 0)
        dcopy(c).start()
        return carry

    lax.fori_loop(0, CQ, middle, 0)

    wsum[...] = jnp.zeros_like(wsum)
    bsum[...] = jnp.zeros_like(bsum)

    def deep(c, carry):
        span = wide(c * 2 * part, 2 * part)
        grad = dpre[span, :]
        full = jnp.concatenate([agg[span, :], other[span, :]], axis=1)
        wsum[...] += lax.dot_general(full, grad, DEEP, preferred_element_type=F32)
        bsum[...] += jnp.sum(grad.astype(F32).reshape(part // 4, 8, width), axis=0)
        return carry

    lax.fori_loop(0, CQ // 2, deep, 0)

    state = {"start": me * 0, "size": high, "at": 0}
    last_bit = nbits - 1

    def sum_start(bit):
        at = state["at"]
        if bit < last_bit:
            half = state["size"] // 2
            upper = (me // (1 << bit)) % 2
            give = state["start"] + (1 - upper) * half
            state["start"] = state["start"] + upper * half
            state["size"] = half
        else:
            half, give = state["size"], state["start"]
        outw[at : at + half] = wsum[wide(give, half)].astype(outw.dtype)
        outgoing = bsum if bit == 0 else btmp.at[2 * bit - 1]
        copies = (
            remote(outw.at[pl.ds(at, half)], inw.at[pl.ds(at, half)], rsend.at[bit], rrecv.at[bit], mate(bit)),
            remote(outgoing, btmp.at[2 * bit], vsend.at[bit], vrecv.at[bit], mate(bit)),
        )
        for copy in copies:
            copy.start()
        return copies

    def sum_end(bit, copies):
        for copy in copies:
            copy.wait()
        half, at = state["size"], state["at"]
        span = wide(state["start"], half)
        came = inw[at : at + half].astype(F32)
        if bit < last_bit:
            wsum[span] += came
        else:
            gath[span] = (outw[at : at + half].astype(F32) + came).astype(gath.dtype)
        outgoing = bsum[...] if bit == 0 else btmp[2 * bit - 1]
        btmp[2 * bit + 1] = outgoing + btmp[2 * bit]
        state["at"] = at + half

    def gather_start(bit):
        span = wide(state["start"], state["size"])
        copy = remote(gath.at[span], gath.at[span], gsend.at[bit], grecv.at[bit], mate(bit))
        copy.start()
        return (copy,)

    def gather_end(bit, copies):
        for copy in copies:
            copy.wait()
        state["start"] = state["start"] - ((me // (1 << bit)) % 2) * state["size"]
        state["size"] = state["size"] * 2

    stages = [(sum_start, sum_end, bit) for bit in range(nbits)]
    stages += [(gather_start, gather_end, bit) for bit in reversed(range(last_bit))]

    flying = stages[0][0](stages[0][2])

    def undo(c, carry):
        dcopy(c).wait()
        span = piece(c)
        both = jnp.concatenate([dpre[span, :], dother[span, :]], axis=1)
        dagg[span, :] = jnp.dot(both, wt[...], preferred_element_type=F32).astype(dagg.dtype)
        return carry

    lax.fori_loop(0, CQ, undo, 0)

    def spread(sources):
        lhs = jnp.concatenate(
            [
                jnp.concatenate([turned[tab[merged + r, s]] for r in range(nblock)], axis=1)
                for s in sources
            ],
            axis=0,
        )
        return jnp.dot(lhs, dagg[...], preferred_element_type=F32)

    boxes = {1: in1, 2: in2}

    def bcopy(m, q):
        return remote(
            bz.at[q, pl.ds((2 - m) * step, step)], boxes[m].at[pl.ds(q * step, step)],
            bsend.at[m - 1, q], brecv.at[m - 1, q], mate(shifts[m]),
        )

    def far_back(q, carry):
        bz[q] = spread(far_sources(q)).astype(bz.dtype).reshape(2 * step, BLK, width)
        bcopy(2, q).start()
        bcopy(1, q).start()
        return carry

    def near_back(i, carry):
        sources = [nblock + i * GROUP + g for g in range(GROUP)]
        b0[pl.ds(i * GROUP, GROUP)] = spread(sources).astype(b0.dtype).reshape(GROUP, BLK, width)
        return carry

    lax.fori_loop(0, nsend // GROUP, near_back, 0)
    ncopy = remote(b0, in0, nsend_sem, nrecv_sem, mate(shifts[0]))

    def own_back(i, carry):
        span = span_of(i)
        acc[span, :] = cotan[span, :].astype(F32) + spread([i * GROUP + g for g in range(GROUP)])
        return carry

    def feed(stage, fed):
        count = FEEDS[stage] if stage < len(FEEDS) else 0
        lax.fori_loop(fed, fed + count, far_back, 0)
        return fed + count

    fed = feed(0, 0)
    lax.fori_loop(0, nsend // GROUP, near_back, 0)
    groups = nblock // GROUP
    for i in range(len(stages)):
        stages[i][1](stages[i][2], flying)
        if i + 1 < len(stages):
            flying = stages[i + 1][0](stages[i + 1][2])
            fed = feed(i + 1, fed)
        if i == 0:
            ncopy.start()
        if i < 2:
            lax.fori_loop(i * groups // 2, (i + 1) * groups // 2, own_back, 0)
        if i == len(stages) - 2:
            ncopy.wait()
    scale = 1.0 / math.sqrt((1 << nbits) * rows)
    dwv[here] = gath[0:width].astype(F32) * scale
    dwv[there] = gath[width : 2 * width].astype(F32) * scale
    db_ref[...] = jnp.sum(btmp[2 * nbits - 1], axis=0, keepdims=True) * scale

    for q in range(ZQ):
        bcopy(2, q).wait()
        bcopy(1, q).wait()


def layer_call(cols, sends, pins, bias, feats, tiles, weight, cotan, shifts, nbits):
    rows, width = feats.shape
    nblock, ntile = cols.shape
    ntiles = nblock * ntile
    high = weight.shape[0]
    nsend = sends.shape[2]
    step = nsend // ZQ
    blocks = feats.reshape(nblock, BLK, width)
    sem = pltpu.SemaphoreType.DMA
    half = feats.dtype
    flat = VMEM((rows, width), half)
    square = VMEM((high, width), half)
    return pl.pallas_call(
        functools.partial(layer_kernel, shifts, nbits),
        in_specs=[VMEM_SPEC, SMEM_SPEC, VMEM_SPEC, VMEM_SPEC] + [HBM_SPEC] * 4,
        out_specs=[VMEM_SPEC] * 7,
        out_shape=[flat, VMEM((rows, width), F32)]
        + [VMEM((nsend, BLK, width), half)] * 3
        + [VMEM((high, width), F32), VMEM((1, width), F32)],
        scratch_shapes=[
            VMEM(blocks.shape, half),
            VMEM((ntiles, BLK, BLK), half),
            VMEM((ntiles + 1, BLK, BLK), half),
            VMEM((ntiles + 1, BLK, BLK), half),
            flat,
            flat,
            VMEM((rows, LANES), F32),
            square,
            VMEM((width, width), half),
            square,
            square,
            VMEM((3, nsend * BLK, width), half),
            VMEM((ZQ, 2 * step * BLK, width), half),
            VMEM((nsend * BLK, width), half),
        ]
        + [flat] * 5
        + [
            VMEM((ZQ, 2 * step, BLK, width), half),
            VMEM((nsend, BLK, width), half),
        ]
        + [VMEM((high, width), F32)]
        + [square] * 3
        + [
            VMEM((8, width), F32),
            VMEM((2 * nbits, 8, width), F32),
            VMEM((3 * nblock, LANES), jnp.int32),
            pltpu.SMEM((3 * nblock, LANES), jnp.int32),
            sem((5,)),
            sem((2, ZQ)),
            sem((2, ZQ)),
            sem,
            sem,
            sem,
            sem,
            sem((CQ,)),
            sem((CQ,)),
            sem((CQ,)),
            sem((CQ,)),
            sem((2, ZQ)),
            sem((2, ZQ)),
            sem,
            sem,
        ]
        + [sem((nbits,))] * 6,
        compiler_params=pltpu.CompilerParams(
            vmem_limit_bytes=52 << 20, collective_id=0, has_side_effects=True
        ),
        name="layer",
    )(cols, sends, pins, bias.reshape(1, width), blocks, tiles.reshape(ntiles, BLK, BLK), weight, cotan)


def join_kernel(sends_ref, out_ref, acc_ref, in0_ref, in1_ref, in2_ref, dw_ref, db_ref, out, dfeat, dw, db, lines, inverse, sems):
    nblock = lines.shape[0]
    nsend, _, width = in0_ref.shape
    copies = [
        pltpu.make_async_copy(out_ref, out, sems.at[0]),
        pltpu.make_async_copy(dw_ref, dw, sems.at[1]),
        pltpu.make_async_copy(db_ref, db, sems.at[2]),
    ]
    for copy in copies:
        copy.start()
    for m in range(3):
        for b in range(nblock):
            inverse[m, b] = nsend
        for j in range(nsend):
            inverse[m, sends_ref[m, 0, j]] = j

    def one_block(b, carry):
        span = pl.ds(pl.multiple_of(b * BLK, BLK), BLK)
        total = acc_ref[span, :]
        for m, ref in enumerate((in0_ref, in1_ref, in2_ref)):
            at = inverse[m, b]
            held = ref[jnp.minimum(at, nsend - 1)].astype(F32)
            total = total + held * jnp.where(at < nsend, 1.0, 0.0)
        lines[b] = total.astype(lines.dtype)
        pltpu.make_async_copy(lines.at[b], dfeat.at[b], sems.at[3 + b]).start()
        return carry

    lax.fori_loop(0, nblock, one_block, 0)
    for b in range(nblock):
        pltpu.make_async_copy(lines.at[b], dfeat.at[b], sems.at[3 + b]).wait()
    for copy in copies:
        copy.wait()


def join_call(sends, out, acc, in0, in1, in2, dw, db):
    rows, width = out.shape
    blocks = (rows // BLK, BLK, width)
    return pl.pallas_call(
        join_kernel,
        in_specs=[SMEM_SPEC] + [VMEM_SPEC] * 7,
        out_specs=[HBM_SPEC] * 4,
        out_shape=[
            jax.ShapeDtypeStruct(out.shape, out.dtype),
            jax.ShapeDtypeStruct(blocks, out.dtype),
            jax.ShapeDtypeStruct(dw.shape, dw.dtype),
            jax.ShapeDtypeStruct(db.shape, db.dtype),
        ],
        scratch_shapes=[
            VMEM(blocks, out.dtype),
            pltpu.SMEM((3, blocks[0]), jnp.int32),
            pltpu.SemaphoreType.DMA((3 + blocks[0],)),
        ],
        compiler_params=pltpu.CompilerParams(vmem_limit_bytes=8 << 20),
        name="join",
    )(sends, out, acc, in0, in1, in2, dw, db)


def body(feats, tiles, tile_cols, sends, pins, weight, bias, cotan):
    nbits = lax.axis_size("dom").bit_length() - 1
    shifts = (0, nbits // 2, nbits - 1)
    sends = jnp.transpose(sends, (1, 0, 2))
    results = layer_call(
        tile_cols, sends, pins, bias, feats, tiles, weight, cotan, shifts, nbits
    )
    out, dfeat, dweight, dbias = join_call(sends, *results)
    return (out, dfeat.reshape(feats.shape), dweight, dbias.reshape(-1))


def solution(mesh):
    return jax.shard_map(
        body,
        mesh=mesh,
        in_specs=(
            P(("basin", "dom"), "hid"),
            P(("basin", "dom"), None, None, None),
            P(("basin", "dom"), None),
            P(("basin", "dom"), None, None),
            P(("basin", "dom"), None),
            P(None, "hid"),
            P("hid"),
            P(("basin", "dom"), "hid"),
        ),
        out_specs=(
            P(("basin", "dom"), "hid"),
            P(("basin", "dom"), "hid"),
            P("basin", "hid"),
            P(("basin", "hid")),
        ),
        check_vma=False,
    )
```

```python
import functools
import math

import jax
import jax.numpy as jnp
from jax import lax
from jax.experimental import pallas as pl
from jax.experimental.pallas import tpu as pltpu
from jax.sharding import PartitionSpec as P

BLK = 128
LANES = 128
ZQ = 8
CQ = 4
GROUP = 4
VMEM = pltpu.VMEM
F32 = jnp.float32

MESH = pl.DeviceIdType.MESH
SMEM_SPEC = pl.BlockSpec(memory_space=pltpu.SMEM)
VMEM_SPEC = pl.BlockSpec(memory_space=pltpu.VMEM)
ANY_SPEC = pl.BlockSpec(memory_space=pl.ANY)
HBM_SPEC = pl.BlockSpec(memory_space=pltpu.HBM)
LAG = 2
FEEDS = (1, 2, 3, 1, 1)

DEEP = (((0,), (0,)), ((), ()))


def flipped(index, bit):
    return index + (1 - 2 * ((index // (1 << bit)) % 2)) * (1 << bit)


def tables(cols):
    nblock, ntile = cols.shape
    lane = lax.broadcasted_iota(jnp.int32, (nblock, LANES), 1)
    row = lax.broadcasted_iota(jnp.int32, (nblock, LANES), 0)
    wide = jnp.concatenate([cols, jnp.full((nblock, LANES - ntile), LANES, jnp.int32)], axis=1)
    one = [jnp.broadcast_to(cols[:, k : k + 1], (nblock, LANES)) for k in range(ntile)]
    rank = jnp.zeros((nblock, LANES), jnp.int32)
    upto = jnp.zeros((nblock, LANES), jnp.int32)
    same = jnp.zeros((nblock, LANES), jnp.int32)
    for k in range(ntile):
        before = (one[k] < wide) | ((one[k] == wide) & (k < lane))
        rank = rank + jnp.where(before, 1, 0)
        upto = upto + jnp.where(one[k] <= lane, 1, 0)
        same = same + jnp.where(one[k] == lane, 1, 0)
    merged = jnp.where(same > 0, row * ntile + upto - 1, nblock * ntile)
    perm = jnp.zeros((nblock, LANES), jnp.int32)
    here = jnp.full((nblock, LANES), -1, jnp.int32)
    prev = jnp.full((nblock, LANES), -2, jnp.int32)
    for k in range(ntile):
        at = jnp.broadcast_to(rank[:, k : k + 1], (nblock, LANES))
        perm = perm + jnp.where(at == lane, row * ntile + k, 0)
        here = jnp.where(at == lane, one[k], here)
        prev = jnp.where(at + 1 == lane, one[k], prev)
    chain = jnp.where(here == prev, 1, 0)
    return jnp.concatenate([perm, chain, merged], axis=0)


def layer_kernel(
    shifts, nbits,
    cols_ref, sends_ref, pins_ref, bias_ref, feats_hbm, tiles_hbm, w_hbm, cotan_hbm,
    outv, acc, in0, in1, in2, dwv, db_ref,
    feats, held, fold, turned, cotan, kcot, keep, w, wx, wp, wt,
    outbox, rz, r0, agg, other, dpre, dother, dagg,
    bz, b0, wsum, outw, inw, gath, bsum, bout, bin_, bfin, tabv, tab,
    fetch_sem, zsend, zrecv, msend, mrecv, xsend, xrecv, asend, arecv, dsend, drecv,
    bsend, brecv, nsend_sem, nrecv_sem, rsend, rrecv, gsend, grecv, vsend, vrecv, hsend, hrecv,
):
    nblock, ntile = cols_ref.shape
    width = feats.shape[2]
    rows = nblock * BLK
    ntiles = nblock * ntile
    high = w.shape[0]
    nsend = sends_ref.shape[2]
    step = nsend // ZQ
    merged = 2 * nblock
    me = lax.axis_index("dom")
    hid = lax.axis_index("hid")
    peer = 1 - hid

    def wide(start, size):
        return pl.ds(pl.multiple_of(start, 16), size)

    here = wide(hid * width, width)
    there = wide(peer * width, width)

    def remote(src, dst, send, recv, where):
        return pltpu.make_async_remote_copy(
            src_ref=src, dst_ref=dst, send_sem=send, recv_sem=recv,
            device_id=where, device_id_type=MESH,
        )

    def mate(bit):
        return {"dom": flipped(me, bit)}

    def lane_mate(bit):
        index = me
        for low in range(1, bit + 1):
            index = flipped(index, low)
        return {"dom": index}

    get_feats = pltpu.make_async_copy(feats_hbm, feats, fetch_sem.at[0])
    get_tiles = pltpu.make_async_copy(tiles_hbm, held, fetch_sem.at[1])
    get_w = pltpu.make_async_copy(w_hbm, w, fetch_sem.at[2])
    get_cotan = pltpu.make_async_copy(cotan_hbm, cotan, fetch_sem.at[3])
    get_feats.start()

    barrier = pltpu.get_barrier_semaphore()
    for bit in range(nbits):
        pl.semaphore_signal(barrier, inc=1, device_id=mate(bit), device_id_type=MESH)
    for bit in range(2, nbits):
        pl.semaphore_signal(barrier, inc=1, device_id=lane_mate(bit), device_id_type=MESH)
    pl.semaphore_signal(barrier, inc=1, device_id={"hid": peer}, device_id_type=MESH)
    get_w.start()
    get_tiles.start()
    get_cotan.start()

    def zcopy(m, q):
        part = pl.ds((2 - m) * step * BLK, step * BLK)
        return remote(
            outbox.at[m, pl.ds(q * step * BLK, step * BLK)], rz.at[q, part],
            zsend.at[m - 1, q], zrecv.at[m - 1, q], mate(shifts[m]),
        )

    def mcopy():
        return remote(outbox.at[0], r0, msend, mrecv, mate(shifts[0]))

    get_feats.wait()
    for m in (2, 1, 0):
        for j in range(nsend):
            outbox[m, j * BLK : (j + 1) * BLK] = feats[sends_ref[m, 0, j]]
    get_w.wait()
    pl.semaphore_wait(barrier, nbits + 1 + max(nbits - 2, 0))
    for q in range(ZQ):
        zcopy(2, q).start()
        zcopy(1, q).start()
        if q == 0:
            mcopy().start()
    wcopy = remote(w.at[there], wx, xsend, xrecv, {"hid": peer})
    wcopy.start()

    tabv[...] = tables(cols_ref[...])
    get_tab = pltpu.make_async_copy(tabv, tab, fetch_sem.at[4])
    get_tab.start()
    fold[ntiles] = jnp.zeros((BLK, BLK), fold.dtype)
    turned[ntiles] = jnp.zeros((BLK, BLK), turned.dtype)
    get_tab.wait()
    get_tiles.wait()

    def fold_row(r, carry):
        total = jnp.zeros((BLK, BLK), F32)
        for n in range(ntile):
            link = tab[nblock + r, n].astype(F32)
            total = total * link + held[tab[r, n]].astype(F32)
            value = total.astype(fold.dtype)
            fold[r * ntile + n] = value
            turned[r * ntile + n] = value.T
        return carry

    lax.fori_loop(0, nblock, fold_row, 0)

    def gathered(i, sources, group=GROUP):
        return jnp.concatenate(
            [
                jnp.concatenate([fold[tab[merged + i * group + g, s]] for s in sources], axis=1)
                for g in range(group)
            ],
            axis=0,
        )

    def span_of(i):
        return wide(i * GROUP * BLK, GROUP * BLK)

    def own_part(i, carry):
        acc[span_of(i), :] = jnp.dot(
            gathered(i, range(nblock)), feats[...].reshape(rows, width), preferred_element_type=F32
        )
        return carry

    lax.fori_loop(0, nblock // GROUP, own_part, 0)

    get_cotan.wait()
    chunk = 512

    def keep_part(i, carry):
        span = wide(i * chunk, chunk)
        ids = lax.broadcasted_iota(jnp.int32, (chunk, pins_ref.shape[1]), 0) + i * chunk
        hit = jnp.where(ids == pins_ref[...], 1.0, 0.0)
        kept = jnp.broadcast_to(1.0 - jnp.max(hit, axis=1, keepdims=True), (chunk, LANES))
        keep[span, :] = kept
        both = jnp.concatenate([kept] * (width // LANES), axis=1)
        kcot[span, :] = (cotan[span, :].astype(F32) * both).astype(kcot.dtype)
        return carry

    lax.fori_loop(0, rows // chunk, keep_part, 0)
    wp[0:width] = w[here, :]
    wp[width : 2 * width] = w[there, :]
    wt[0:width] = w[here, :].T
    wcopy.wait()
    wt[width : 2 * width] = wx[...].T

    mcopy().wait()

    def near_part(i, carry):
        acc[span_of(i), :] += jnp.dot(
            gathered(i, range(nblock, nblock + nsend)), r0[...], preferred_element_type=F32
        )
        return carry

    lax.fori_loop(0, nblock // GROUP, near_part, 0)

    def far_sources(q):
        return [nblock + m * nsend + q * step + j for m in (2, 1) for j in range(step)]

    def far_part(q, i):
        return acc[span_of(i), :] + jnp.dot(
            gathered(i, far_sources(q)), rz[q], preferred_element_type=F32
        )

    for q in range(ZQ - 1):
        zcopy(2, q).wait()
        zcopy(1, q).wait()

        def some_part(i, carry, q=q):
            acc[span_of(i), :] = far_part(q, i)
            return carry

        lax.fori_loop(0, nblock // GROUP, some_part, 0)

    part = rows // CQ
    inch = min(part, 512)
    deep_rows = rows // 2

    def piece(c):
        return wide(c * part, part)

    def acopy(c):
        return remote(
            agg.at[piece(c)], other.at[piece(c)], asend.at[c], arecv.at[c], {"hid": peer}
        )

    def dcopy(c):
        return remote(
            dpre.at[piece(c)], dother.at[piece(c)], dsend.at[c], drecv.at[c], {"hid": peer}
        )

    zcopy(2, ZQ - 1).wait()
    zcopy(1, ZQ - 1).wait()

    def last_part(i, carry):
        final = acc[piece(i), :] + jnp.dot(
            gathered(i, far_sources(ZQ - 1), nblock // CQ), rz[ZQ - 1], preferred_element_type=F32
        )
        agg[piece(i), :] = final.astype(agg.dtype)
        acopy(i).start()
        return carry

    lax.fori_loop(0, CQ, last_part, 0)

    def middle(c, carry):
        acopy(c).wait()

        def inner(i, carry):
            span = wide(c * part + i * inch, inch)
            full = jnp.concatenate([agg[span, :], other[span, :]], axis=1)
            pre = jnp.dot(full, wp[...], preferred_element_type=F32) + bias_ref[...]
            both = jnp.concatenate([keep[span, :]] * (width // LANES), axis=1)
            sig = jax.nn.sigmoid(pre)
            gate = pre * sig
            at = pl.ds(c * (part // BLK) + i * (inch // BLK), inch // BLK)
            old = feats[at].reshape(inch, width).astype(F32)
            outv[span, :] = (old + both * gate).astype(outv.dtype)
            dpre[span, :] = (
                kcot[span, :].astype(F32) * (sig * (1.0 + pre * (1.0 - sig)))
            ).astype(dpre.dtype)
            return carry

        lax.fori_loop(0, part // inch, inner, 0)
        dcopy(c).start()
        return carry

    lax.fori_loop(0, CQ, middle, 0)

    wsum[...] = jnp.zeros_like(wsum)
    bsum[...] = jnp.zeros_like(bsum)

    def deep(c, carry):
        span = wide(c * deep_rows, deep_rows)
        grad = dpre[span, :]
        full = jnp.concatenate([agg[span, :], other[span, :]], axis=1)
        wsum[...] += lax.dot_general(full, grad, DEEP, preferred_element_type=F32)
        bsum[...] += jnp.sum(grad.astype(F32).reshape(deep_rows // 8, 8, width), axis=0)
        return carry

    lax.fori_loop(0, rows // deep_rows, deep, 0)

    half = high // 2
    last_bit = nbits - 1

    def digit(bit):
        return (me // (1 << bit)) % 2

    lower = wide(digit(0) * half, half)
    upper = wide((1 - digit(0)) * half, half)

    def differ(bit):
        return digit(bit) != digit(bit + 1)

    def taking(bit):
        on = me >= 0
        for low in range(1, bit):
            on = on & differ(low)
        return on

    def half_copies(bit):
        where = mate(0) if bit == 0 else lane_mate(bit)
        return (
            remote(outw.at[bit], inw.at[bit], rsend.at[bit], rrecv.at[bit], where),
            remote(bout.at[bit], bin_.at[bit], vsend.at[bit], vrecv.at[bit], where),
        )

    def sum_start(bit):
        def go():
            outw[bit] = wsum[upper if bit == 0 else lower].astype(outw.dtype)
            bout[bit] = bsum[...]
            for copy in half_copies(bit):
                copy.start()

        if bit == 0:
            go()
        elif bit == last_bit:
            pl.when(taking(bit))(go)
        else:
            pl.when(taking(bit) & jnp.logical_not(differ(bit)))(go)

    def sum_end(bit):
        def come():
            for copy in half_copies(bit):
                copy.wait_recv()
            if bit == last_bit:
                both = outw[bit].astype(F32) + inw[bit].astype(F32)
                gath[lower] = both.astype(gath.dtype)
                bfin[...] = bout[bit] + bin_[bit]
            else:
                wsum[lower] += inw[bit].astype(F32)
                bsum[...] += bin_[bit]

        if bit == 0:
            come()
        elif bit == last_bit:
            pl.when(taking(bit))(come)
        else:
            pl.when(taking(bit) & differ(bit))(come)

    def back_copies(bit):
        return (
            remote(gath.at[lower], gath.at[lower], gsend.at[bit], grecv.at[bit], lane_mate(bit)),
            remote(bfin, bfin, hsend.at[bit], hrecv.at[bit], lane_mate(bit)),
        )

    def side_copy():
        return remote(gath.at[lower], gath.at[lower], gsend.at[0], grecv.at[0], mate(0))

    def back_start(bit):
        if bit == 0:
            side_copy().start()
            return

        def go():
            for copy in back_copies(bit):
                copy.start()

        pl.when(taking(bit) & differ(bit))(go)

    def back_end(bit):
        if bit == 0:
            side_copy().wait()
            return

        def come():
            for copy in back_copies(bit):
                copy.wait_recv()

        pl.when(taking(bit) & jnp.logical_not(differ(bit)))(come)

    boxes = {1: in1, 2: in2}

    def bcopy(m, q):
        return remote(
            bz.at[q, pl.ds((2 - m) * step, step)], boxes[m].at[pl.ds(q * step, step)],
            bsend.at[m - 1, q], brecv.at[m - 1, q], mate(shifts[m]),
        )

    def idle(bit):
        on = taking(bit) if bit == last_bit else taking(bit) & differ(bit)
        return jnp.logical_not(on)

    paced = {}

    def pace(bit, piece_at):
        paced[piece_at] = bit

        def hold():
            bcopy(2, piece_at).wait()
            bcopy(1, piece_at).wait()

        pl.when(idle(bit))(hold)

    def drain():
        for bit in range(nbits):
            def sent(bit=bit):
                for copy in half_copies(bit):
                    copy.wait_send()

            if bit == 0:
                sent()
            elif bit == last_bit:
                pl.when(taking(bit))(sent)
            else:
                pl.when(taking(bit) & jnp.logical_not(differ(bit)))(sent)
        for bit in range(1, last_bit):
            def given(bit=bit):
                for copy in back_copies(bit):
                    copy.wait_send()

            pl.when(taking(bit) & differ(bit))(given)

    stages = [(sum_start, sum_end, bit) for bit in range(nbits)]
    stages += [(back_start, back_end, bit) for bit in reversed(range(last_bit))]

    stages[0][0](stages[0][2])

    def undo(c, carry):
        dcopy(c).wait()
        span = piece(c)
        both = jnp.concatenate([dpre[span, :], dother[span, :]], axis=1)
        dagg[span, :] = jnp.dot(both, wt[...], preferred_element_type=F32).astype(dagg.dtype)
        return carry

    lax.fori_loop(0, CQ, undo, 0)

    def spread(sources):
        lhs = jnp.concatenate(
            [
                jnp.concatenate([turned[tab[merged + r, s]] for r in range(nblock)], axis=1)
                for s in sources
            ],
            axis=0,
        )
        return jnp.dot(lhs, dagg[...], preferred_element_type=F32)

    def far_back(q, carry):
        bz[q] = spread(far_sources(q)).astype(bz.dtype).reshape(2 * step, BLK, width)
        bcopy(2, q).start()
        bcopy(1, q).start()
        return carry

    def near_back(i, carry):
        sources = [nblock + i * GROUP + g for g in range(GROUP)]
        b0[pl.ds(i * GROUP, GROUP)] = spread(sources).astype(b0.dtype).reshape(GROUP, BLK, width)
        return carry

    lax.fori_loop(0, nsend // GROUP, near_back, 0)
    ncopy = remote(b0, in0, nsend_sem, nrecv_sem, mate(shifts[0]))

    def own_back(i, carry):
        span = span_of(i)
        acc[span, :] = cotan[span, :].astype(F32) + spread([i * GROUP + g for g in range(GROUP)])
        return carry

    def feed(stage, fed):
        count = FEEDS[stage] if stage < len(FEEDS) else 0
        lax.fori_loop(fed, fed + count, far_back, 0)
        return fed + count

    fed = feed(0, 0)
    lax.fori_loop(0, nsend // GROUP, near_back, 0)
    groups = nblock // GROUP
    for i in range(len(stages)):
        stages[i][1](stages[i][2])
        if 0 < i < nbits and LAG <= fed < ZQ and fed - LAG not in paced:
            pace(i, fed - LAG)
        if i + 1 < len(stages):
            stages[i + 1][0](stages[i + 1][2])
            fed = feed(i + 1, fed)
        if i == 0:
            ncopy.start()
        if i < 2:
            lax.fori_loop(i * groups // 2, (i + 1) * groups // 2, own_back, 0)
        if i == len(stages) - 2:
            ncopy.wait()
    scale = 1.0 / math.sqrt((1 << nbits) * rows)
    dwv[here] = gath[0:width].astype(F32) * scale
    dwv[there] = gath[width : 2 * width].astype(F32) * scale
    db_ref[...] = jnp.sum(bfin[...], axis=0, keepdims=True) * scale
    drain()

    for q in range(ZQ):
        def landed(q=q):
            bcopy(2, q).wait()
            bcopy(1, q).wait()

        if q in paced:
            pl.when(jnp.logical_not(idle(paced[q])))(landed)
        else:
            landed()


def layer_call(cols, sends, pins, bias, feats, tiles, weight, cotan, shifts, nbits):
    rows, width = feats.shape
    nblock, ntile = cols.shape
    ntiles = nblock * ntile
    high = weight.shape[0]
    nsend = sends.shape[2]
    step = nsend // ZQ
    blocks = feats.reshape(nblock, BLK, width)
    sem = pltpu.SemaphoreType.DMA
    half = feats.dtype
    flat = VMEM((rows, width), half)
    square = VMEM((high, width), half)
    return pl.pallas_call(
        functools.partial(layer_kernel, shifts, nbits),
        in_specs=[VMEM_SPEC, SMEM_SPEC, VMEM_SPEC, VMEM_SPEC] + [HBM_SPEC] * 4,
        out_specs=[VMEM_SPEC] * 7,
        out_shape=[flat, VMEM((rows, width), F32)]
        + [VMEM((nsend, BLK, width), half)] * 3
        + [VMEM((high, width), F32), VMEM((1, width), F32)],
        scratch_shapes=[
            VMEM(blocks.shape, half),
            VMEM((ntiles, BLK, BLK), half),
            VMEM((ntiles + 1, BLK, BLK), half),
            VMEM((ntiles + 1, BLK, BLK), half),
            flat,
            flat,
            VMEM((rows, LANES), F32),
            square,
            VMEM((width, width), half),
            square,
            square,
            VMEM((3, nsend * BLK, width), half),
            VMEM((ZQ, 2 * step * BLK, width), half),
            VMEM((nsend * BLK, width), half),
        ]
        + [flat] * 5
        + [
            VMEM((ZQ, 2 * step, BLK, width), half),
            VMEM((nsend, BLK, width), half),
        ]
        + [VMEM((high, width), F32)]
        + [VMEM((nbits, high // 2, width), half)] * 2
        + [
            square,
            VMEM((8, width), F32),
            VMEM((nbits, 8, width), F32),
            VMEM((nbits, 8, width), F32),
            VMEM((8, width), F32),
            VMEM((3 * nblock, LANES), jnp.int32),
            pltpu.SMEM((3 * nblock, LANES), jnp.int32),
            sem((5,)),
            sem((2, ZQ)),
            sem((2, ZQ)),
            sem,
            sem,
            sem,
            sem,
            sem((CQ,)),
            sem((CQ,)),
            sem((CQ,)),
            sem((CQ,)),
            sem((2, ZQ)),
            sem((2, ZQ)),
            sem,
            sem,
        ]
        + [sem((nbits,))] * 8,
        compiler_params=pltpu.CompilerParams(
            vmem_limit_bytes=52 << 20, collective_id=0, has_side_effects=True
        ),
        name="layer",
    )(cols, sends, pins, bias.reshape(1, width), blocks, tiles.reshape(ntiles, BLK, BLK), weight, cotan)


def join_kernel(sends_any, out_ref, acc_ref, in0_ref, in1_ref, in2_ref, dw_ref, db_ref, out, dfeat, dw, db, lines, sends_ref, inverse, sems):
    nblock = lines.shape[0]
    nsend, _, width = in0_ref.shape
    copies = [
        pltpu.make_async_copy(out_ref, out, sems.at[0]),
        pltpu.make_async_copy(dw_ref, dw, sems.at[1]),
        pltpu.make_async_copy(db_ref, db, sems.at[2]),
    ]
    get_sends = pltpu.make_async_copy(sends_any, sends_ref, sems.at[3 + nblock])
    get_sends.start()
    for copy in copies:
        copy.start()
    get_sends.wait()
    for m in range(3):
        for b in range(nblock):
            inverse[m, b] = nsend
        for j in range(nsend):
            inverse[m, sends_ref[m, 0, j]] = j

    def one_block(b, carry):
        span = pl.ds(pl.multiple_of(b * BLK, BLK), BLK)
        total = acc_ref[span, :]
        for m, ref in enumerate((in0_ref, in1_ref, in2_ref)):
            at = inverse[m, b]
            held = ref[jnp.minimum(at, nsend - 1)].astype(F32)
            total = total + held * jnp.where(at < nsend, 1.0, 0.0)
        lines[b] = total.astype(lines.dtype)
        pltpu.make_async_copy(lines.at[b], dfeat.at[b], sems.at[3 + b]).start()
        return carry

    lax.fori_loop(0, nblock, one_block, 0, unroll=2)
    for b in range(nblock):
        pltpu.make_async_copy(lines.at[b], dfeat.at[b], sems.at[3 + b]).wait()
    for copy in copies:
        copy.wait()


def join_call(sends, out, acc, in0, in1, in2, dw, db):
    rows, width = out.shape
    blocks = (rows // BLK, BLK, width)
    return pl.pallas_call(
        join_kernel,
        in_specs=[ANY_SPEC] + [VMEM_SPEC] * 7,
        out_specs=[HBM_SPEC] * 4,
        out_shape=[
            jax.ShapeDtypeStruct(out.shape, out.dtype),
            jax.ShapeDtypeStruct(blocks, out.dtype),
            jax.ShapeDtypeStruct(dw.shape, dw.dtype),
            jax.ShapeDtypeStruct(db.shape, db.dtype),
        ],
        scratch_shapes=[
            VMEM(blocks, out.dtype),
            pltpu.SMEM(sends.shape, jnp.int32),
            pltpu.SMEM((3, blocks[0]), jnp.int32),
            pltpu.SemaphoreType.DMA((4 + blocks[0],)),
        ],
        compiler_params=pltpu.CompilerParams(vmem_limit_bytes=8 << 20),
        name="join",
    )(sends, out, acc, in0, in1, in2, dw, db)


def body(feats, tiles, tile_cols, sends, pins, weight, bias, cotan):
    nbits = lax.axis_size("dom").bit_length() - 1
    shifts = (0, nbits // 2, nbits - 1)
    sends = jnp.transpose(sends, (1, 0, 2))
    results = layer_call(
        tile_cols, sends, pins, bias, feats, tiles, weight, cotan, shifts, nbits
    )
    out, dfeat, dweight, dbias = join_call(sends, *results)
    return (out, dfeat.reshape(feats.shape), dweight, dbias.reshape(-1))


def solution(mesh):
    return jax.shard_map(
        body,
        mesh=mesh,
        in_specs=(
            P(("basin", "dom"), "hid"),
            P(("basin", "dom"), None, None, None),
            P(("basin", "dom"), None),
            P(("basin", "dom"), None, None),
            P(("basin", "dom"), None),
            P(None, "hid"),
            P("hid"),
            P(("basin", "dom"), "hid"),
        ),
        out_specs=(
            P(("basin", "dom"), "hid"),
            P(("basin", "dom"), "hid"),
            P("basin", "hid"),
            P(("basin", "hid")),
        ),
        check_vma=False,
    )
```

```python
import functools
import math

import jax
import jax.numpy as jnp
from jax import lax
from jax.experimental import pallas as pl
from jax.experimental.pallas import tpu as pltpu
from jax.sharding import PartitionSpec as P

BLK = 128
LANES = 128
ZQ = 8
CQ = 4
GROUP = 4
VMEM = pltpu.VMEM
F32 = jnp.float32

MESH = pl.DeviceIdType.MESH
SMEM_SPEC = pl.BlockSpec(memory_space=pltpu.SMEM)
VMEM_SPEC = pl.BlockSpec(memory_space=pltpu.VMEM)
ANY_SPEC = pl.BlockSpec(memory_space=pl.ANY)
HBM_SPEC = pl.BlockSpec(memory_space=pltpu.HBM)
LAG = 2
FEEDS = (1, 2, 3, 1, 1)

DEEP = (((0,), (0,)), ((), ()))


def flipped(index, bit):
    return index + (1 - 2 * ((index // (1 << bit)) % 2)) * (1 << bit)


def tables(cols):
    nblock, ntile = cols.shape
    lane = lax.broadcasted_iota(jnp.int32, (nblock, LANES), 1)
    row = lax.broadcasted_iota(jnp.int32, (nblock, LANES), 0)
    wide = jnp.concatenate([cols, jnp.full((nblock, LANES - ntile), LANES, jnp.int32)], axis=1)
    one = [jnp.broadcast_to(cols[:, k : k + 1], (nblock, LANES)) for k in range(ntile)]
    rank = jnp.zeros((nblock, LANES), jnp.int32)
    upto = jnp.zeros((nblock, LANES), jnp.int32)
    same = jnp.zeros((nblock, LANES), jnp.int32)
    for k in range(ntile):
        before = (one[k] < wide) | ((one[k] == wide) & (k < lane))
        rank = rank + jnp.where(before, 1, 0)
        upto = upto + jnp.where(one[k] <= lane, 1, 0)
        same = same + jnp.where(one[k] == lane, 1, 0)
    merged = jnp.where(same > 0, row * ntile + upto - 1, nblock * ntile)
    perm = jnp.zeros((nblock, LANES), jnp.int32)
    here = jnp.full((nblock, LANES), -1, jnp.int32)
    prev = jnp.full((nblock, LANES), -2, jnp.int32)
    for k in range(ntile):
        at = jnp.broadcast_to(rank[:, k : k + 1], (nblock, LANES))
        perm = perm + jnp.where(at == lane, row * ntile + k, 0)
        here = jnp.where(at == lane, one[k], here)
        prev = jnp.where(at + 1 == lane, one[k], prev)
    chain = jnp.where(here == prev, 1, 0)
    return jnp.concatenate([perm, chain, merged], axis=0)


def layer_kernel(
    shifts, nbits,
    cols_hbm, sends_hbm, pins_hbm, bias_hbm, feats_hbm, tiles_hbm, w_hbm, cotan_hbm,
    outv, acc, in0, in1, in2, dwv, db_ref,
    cols_ref, sends_ref, pins_ref, bias_ref, feats, held, fold, turned, cotan, kcot, keep, w, wx, wp, wt,
    outbox, rz, r0, agg, other, dpre, dother, dagg,
    bz, b0, wsum, outw, inw, gath, bsum, bout, bin_, bfin, tabv, tab,
    fetch_sem, zsend, zrecv, msend, mrecv, xsend, xrecv, asend, arecv, dsend, drecv,
    bsend, brecv, nsend_sem, nrecv_sem, rsend, rrecv, gsend, grecv, vsend, vrecv, hsend, hrecv,
):
    nblock, ntile = cols_ref.shape
    width = feats.shape[2]
    rows = nblock * BLK
    ntiles = nblock * ntile
    high = w.shape[0]
    nsend = sends_ref.shape[2]
    step = nsend // ZQ
    merged = 2 * nblock
    me = lax.axis_index("dom")
    hid = lax.axis_index("hid")
    peer = 1 - hid

    def wide(start, size):
        return pl.ds(pl.multiple_of(start, 16), size)

    here = wide(hid * width, width)
    there = wide(peer * width, width)

    def remote(src, dst, send, recv, where):
        return pltpu.make_async_remote_copy(
            src_ref=src, dst_ref=dst, send_sem=send, recv_sem=recv,
            device_id=where, device_id_type=MESH,
        )

    def mate(bit):
        return {"dom": flipped(me, bit)}

    def lane_mate(bit):
        index = me
        for low in range(1, bit + 1):
            index = flipped(index, low)
        return {"dom": index}

    get_feats = pltpu.make_async_copy(feats_hbm, feats, fetch_sem.at[0])
    get_tiles = pltpu.make_async_copy(tiles_hbm, held, fetch_sem.at[1])
    get_w = pltpu.make_async_copy(w_hbm, w, fetch_sem.at[2])
    get_cotan = pltpu.make_async_copy(cotan_hbm, cotan, fetch_sem.at[3])
    small = (
        (sends_hbm, sends_ref), (cols_hbm, cols_ref), (pins_hbm, pins_ref), (bias_hbm, bias_ref),
    )
    get_small = [
        pltpu.make_async_copy(src, dst, fetch_sem.at[5 + i]) for i, (src, dst) in enumerate(small)
    ]

    barrier = pltpu.get_barrier_semaphore()
    for bit in reversed(range(nbits)):
        pl.semaphore_signal(barrier, inc=1, device_id=mate(bit), device_id_type=MESH)
    for bit in range(2, nbits):
        pl.semaphore_signal(barrier, inc=1, device_id=lane_mate(bit), device_id_type=MESH)
    pl.semaphore_signal(barrier, inc=1, device_id={"hid": peer}, device_id_type=MESH)
    for copy in get_small:
        copy.start()
    get_feats.start()
    get_w.start()
    get_tiles.start()
    get_cotan.start()

    def zcopy(m, q):
        part = pl.ds((2 - m) * step * BLK, step * BLK)
        return remote(
            outbox.at[m, pl.ds(q * step * BLK, step * BLK)], rz.at[q, part],
            zsend.at[m - 1, q], zrecv.at[m - 1, q], mate(shifts[m]),
        )

    def mcopy():
        return remote(outbox.at[0], r0, msend, mrecv, mate(shifts[0]))

    for copy in get_small:
        copy.wait()
    get_feats.wait()
    for m in (2, 1, 0):
        for j in range(nsend):
            outbox[m, j * BLK : (j + 1) * BLK] = feats[sends_ref[m, 0, j]]
    get_w.wait()
    pl.semaphore_wait(barrier, nbits + 1 + max(nbits - 2, 0))
    for q in range(ZQ):
        zcopy(2, q).start()
        zcopy(1, q).start()
        if q == 0:
            mcopy().start()
    wcopy = remote(w.at[there], wx, xsend, xrecv, {"hid": peer})
    wcopy.start()

    tabv[...] = tables(cols_ref[...])
    get_tab = pltpu.make_async_copy(tabv, tab, fetch_sem.at[4])
    get_tab.start()
    fold[ntiles] = jnp.zeros((BLK, BLK), fold.dtype)
    turned[ntiles] = jnp.zeros((BLK, BLK), turned.dtype)
    get_tab.wait()
    get_tiles.wait()

    def fold_row(r, carry):
        total = jnp.zeros((BLK, BLK), F32)
        for n in range(ntile):
            link = tab[nblock + r, n].astype(F32)
            total = total * link + held[tab[r, n]].astype(F32)
            value = total.astype(fold.dtype)
            fold[r * ntile + n] = value
            turned[r * ntile + n] = value.T
        return carry

    lax.fori_loop(0, nblock, fold_row, 0)

    def gathered(i, sources, group=GROUP):
        return jnp.concatenate(
            [
                jnp.concatenate([fold[tab[merged + i * group + g, s]] for s in sources], axis=1)
                for g in range(group)
            ],
            axis=0,
        )

    def span_of(i):
        return wide(i * GROUP * BLK, GROUP * BLK)

    def own_part(i, carry):
        acc[span_of(i), :] = jnp.dot(
            gathered(i, range(nblock)), feats[...].reshape(rows, width), preferred_element_type=F32
        )
        return carry

    lax.fori_loop(0, nblock // GROUP, own_part, 0)

    get_cotan.wait()
    chunk = 512

    def keep_part(i, carry):
        span = wide(i * chunk, chunk)
        ids = lax.broadcasted_iota(jnp.int32, (chunk, pins_ref.shape[1]), 0) + i * chunk
        hit = jnp.where(ids == pins_ref[...], 1.0, 0.0)
        kept = jnp.broadcast_to(1.0 - jnp.max(hit, axis=1, keepdims=True), (chunk, LANES))
        keep[span, :] = kept
        both = jnp.concatenate([kept] * (width // LANES), axis=1)
        kcot[span, :] = (cotan[span, :].astype(F32) * both).astype(kcot.dtype)
        return carry

    lax.fori_loop(0, rows // chunk, keep_part, 0)
    wp[0:width] = w[here, :]
    wp[width : 2 * width] = w[there, :]
    wt[0:width] = w[here, :].T
    wcopy.wait()
    wt[width : 2 * width] = wx[...].T

    mcopy().wait()

    def near_part(i, carry):
        acc[span_of(i), :] += jnp.dot(
            gathered(i, range(nblock, nblock + nsend)), r0[...], preferred_element_type=F32
        )
        return carry

    lax.fori_loop(0, nblock // GROUP, near_part, 0)

    def far_sources(q):
        return [nblock + m * nsend + q * step + j for m in (2, 1) for j in range(step)]

    def far_part(q, i):
        return acc[span_of(i), :] + jnp.dot(
            gathered(i, far_sources(q)), rz[q], preferred_element_type=F32
        )

    for q in range(ZQ - 1):
        zcopy(2, q).wait()
        zcopy(1, q).wait()

        def some_part(i, carry, q=q):
            acc[span_of(i), :] = far_part(q, i)
            return carry

        lax.fori_loop(0, nblock // GROUP, some_part, 0)

    part = rows // CQ
    inch = min(part, 512)
    deep_rows = rows

    def piece(c):
        return wide(c * part, part)

    def acopy(c):
        return remote(
            agg.at[piece(c)], other.at[piece(c)], asend.at[c], arecv.at[c], {"hid": peer}
        )

    def dcopy(c):
        return remote(
            dpre.at[piece(c)], dother.at[piece(c)], dsend.at[c], drecv.at[c], {"hid": peer}
        )

    zcopy(2, ZQ - 1).wait()
    zcopy(1, ZQ - 1).wait()

    def last_part(i, carry):
        final = acc[piece(i), :] + jnp.dot(
            gathered(i, far_sources(ZQ - 1), nblock // CQ), rz[ZQ - 1], preferred_element_type=F32
        )
        agg[piece(i), :] = final.astype(agg.dtype)
        acopy(i).start()
        return carry

    lax.fori_loop(0, CQ, last_part, 0)

    def middle(c, carry):
        acopy(c).wait()

        def inner(i, carry):
            span = wide(c * part + i * inch, inch)
            full = jnp.concatenate([agg[span, :], other[span, :]], axis=1)
            pre = jnp.dot(full, wp[...], preferred_element_type=F32) + bias_ref[...]
            both = jnp.concatenate([keep[span, :]] * (width // LANES), axis=1)
            sig = jax.nn.sigmoid(pre)
            gate = pre * sig
            at = pl.ds(c * (part // BLK) + i * (inch // BLK), inch // BLK)
            old = feats[at].reshape(inch, width).astype(F32)
            outv[span, :] = (old + both * gate).astype(outv.dtype)
            dpre[span, :] = (
                kcot[span, :].astype(F32) * (sig * (1.0 + pre * (1.0 - sig)))
            ).astype(dpre.dtype)
            return carry

        lax.fori_loop(0, part // inch, inner, 0)
        dcopy(c).start()
        return carry

    lax.fori_loop(0, CQ, middle, 0)

    wsum[...] = jnp.zeros_like(wsum)
    bsum[...] = jnp.zeros_like(bsum)

    def deep(c, carry):
        span = wide(c * deep_rows, deep_rows)
        grad = dpre[span, :]
        full = jnp.concatenate([agg[span, :], other[span, :]], axis=1)
        wsum[...] += lax.dot_general(full, grad, DEEP, preferred_element_type=F32)
        bsum[...] += jnp.sum(grad.astype(F32).reshape(deep_rows // 8, 8, width), axis=0)
        return carry

    lax.fori_loop(0, rows // deep_rows, deep, 0)

    half = high // 2
    last_bit = nbits - 1

    def digit(bit):
        return (me // (1 << bit)) % 2

    lower = wide(digit(0) * half, half)
    upper = wide((1 - digit(0)) * half, half)

    def differ(bit):
        return digit(bit) != digit(bit + 1)

    def taking(bit):
        on = me >= 0
        for low in range(1, bit):
            on = on & differ(low)
        return on

    def half_copies(bit):
        where = mate(0) if bit == 0 else lane_mate(bit)
        return (
            remote(outw.at[bit], inw.at[bit], rsend.at[bit], rrecv.at[bit], where),
            remote(bout.at[bit], bin_.at[bit], vsend.at[bit], vrecv.at[bit], where),
        )

    def sum_start(bit):
        def go():
            outw[bit] = wsum[upper if bit == 0 else lower].astype(outw.dtype)
            bout[bit] = bsum[...]
            for copy in half_copies(bit):
                copy.start()

        if bit == 0:
            go()
        elif bit == last_bit:
            pl.when(taking(bit))(go)
        else:
            pl.when(taking(bit) & jnp.logical_not(differ(bit)))(go)

    def sum_end(bit):
        def come():
            for copy in half_copies(bit):
                copy.wait_recv()
            if bit == last_bit:
                both = outw[bit].astype(F32) + inw[bit].astype(F32)
                gath[lower] = both.astype(gath.dtype)
                bfin[...] = bout[bit] + bin_[bit]
            else:
                wsum[lower] += inw[bit].astype(F32)
                bsum[...] += bin_[bit]

        if bit == 0:
            come()
        elif bit == last_bit:
            pl.when(taking(bit))(come)
        else:
            pl.when(taking(bit) & differ(bit))(come)

    def back_copies(bit):
        return (
            remote(gath.at[lower], gath.at[lower], gsend.at[bit], grecv.at[bit], lane_mate(bit)),
            remote(bfin, bfin, hsend.at[bit], hrecv.at[bit], lane_mate(bit)),
        )

    def side_copy():
        return remote(gath.at[lower], gath.at[lower], gsend.at[0], grecv.at[0], mate(0))

    def back_start(bit):
        if bit == 0:
            side_copy().start()
            return

        def go():
            for copy in back_copies(bit):
                copy.start()

        pl.when(taking(bit) & differ(bit))(go)

    def back_end(bit):
        if bit == 0:
            side_copy().wait()
            return

        def come():
            for copy in back_copies(bit):
                copy.wait_recv()

        pl.when(taking(bit) & jnp.logical_not(differ(bit)))(come)

    boxes = {1: in1, 2: in2}

    def bcopy(m, q):
        return remote(
            bz.at[q, pl.ds((2 - m) * step, step)], boxes[m].at[pl.ds(q * step, step)],
            bsend.at[m - 1, q], brecv.at[m - 1, q], mate(shifts[m]),
        )

    def idle(bit):
        on = taking(bit) if bit == last_bit else taking(bit) & differ(bit)
        return jnp.logical_not(on)

    paced = {}

    def pace(bit, piece_at):
        paced[piece_at] = bit

        def hold():
            bcopy(2, piece_at).wait()
            bcopy(1, piece_at).wait()

        pl.when(idle(bit))(hold)

    def drain():
        for bit in range(nbits):
            def sent(bit=bit):
                for copy in half_copies(bit):
                    copy.wait_send()

            if bit == 0:
                sent()
            elif bit == last_bit:
                pl.when(taking(bit))(sent)
            else:
                pl.when(taking(bit) & jnp.logical_not(differ(bit)))(sent)
        for bit in range(1, last_bit):
            def given(bit=bit):
                for copy in back_copies(bit):
                    copy.wait_send()

            pl.when(taking(bit) & differ(bit))(given)

    stages = [(sum_start, sum_end, bit) for bit in range(nbits)]
    stages += [(back_start, back_end, bit) for bit in reversed(range(last_bit))]

    stages[0][0](stages[0][2])

    def undo(c, carry):
        dcopy(2 * c).wait()
        dcopy(2 * c + 1).wait()
        span = wide(c * 2 * part, 2 * part)
        both = jnp.concatenate([dpre[span, :], dother[span, :]], axis=1)
        dagg[span, :] = jnp.dot(both, wt[...], preferred_element_type=F32).astype(dagg.dtype)
        return carry

    lax.fori_loop(0, CQ // 2, undo, 0)

    def spread(sources):
        lhs = jnp.concatenate(
            [
                jnp.concatenate([turned[tab[merged + r, s]] for r in range(nblock)], axis=1)
                for s in sources
            ],
            axis=0,
        )
        return jnp.dot(lhs, dagg[...], preferred_element_type=F32)

    def far_back(q, carry):
        bz[q] = spread(far_sources(q)).astype(bz.dtype).reshape(2 * step, BLK, width)
        bcopy(2, q).start()
        bcopy(1, q).start()
        return carry

    def near_back(i, carry):
        sources = [nblock + i * GROUP + g for g in range(GROUP)]
        b0[pl.ds(i * GROUP, GROUP)] = spread(sources).astype(b0.dtype).reshape(GROUP, BLK, width)
        return carry

    lax.fori_loop(0, nsend // GROUP, near_back, 0)
    ncopy = remote(b0, in0, nsend_sem, nrecv_sem, mate(shifts[0]))

    def own_back(i, carry):
        span = span_of(i)
        acc[span, :] = cotan[span, :].astype(F32) + spread([i * GROUP + g for g in range(GROUP)])
        return carry

    def feed(stage, fed):
        count = FEEDS[stage] if stage < len(FEEDS) else 0
        lax.fori_loop(fed, fed + count, far_back, 0)
        return fed + count

    fed = feed(0, 0)
    lax.fori_loop(0, nsend // GROUP, near_back, 0)
    groups = nblock // GROUP
    for i in range(len(stages)):
        stages[i][1](stages[i][2])
        if 0 < i < nbits and LAG <= fed < ZQ and fed - LAG not in paced:
            pace(i, fed - LAG)
        if i + 1 < len(stages):
            stages[i + 1][0](stages[i + 1][2])
            fed = feed(i + 1, fed)
        if i == 0:
            ncopy.start()
        if i < 2:
            lax.fori_loop(i * groups // 2, (i + 1) * groups // 2, own_back, 0)
        if i == len(stages) - 2:
            ncopy.wait()
    scale = 1.0 / math.sqrt((1 << nbits) * rows)
    dwv[here] = gath[0:width].astype(F32) * scale
    dwv[there] = gath[width : 2 * width].astype(F32) * scale
    db_ref[...] = jnp.sum(bfin[...], axis=0, keepdims=True) * scale
    drain()

    for q in range(ZQ):
        def landed(q=q):
            bcopy(2, q).wait()
            bcopy(1, q).wait()

        if q in paced:
            pl.when(jnp.logical_not(idle(paced[q])))(landed)
        else:
            landed()


def layer_call(cols, sends, pins, bias, feats, tiles, weight, cotan, shifts, nbits):
    rows, width = feats.shape
    nblock, ntile = cols.shape
    ntiles = nblock * ntile
    high = weight.shape[0]
    nsend = sends.shape[2]
    step = nsend // ZQ
    blocks = feats.reshape(nblock, BLK, width)
    sem = pltpu.SemaphoreType.DMA
    half = feats.dtype
    flat = VMEM((rows, width), half)
    square = VMEM((high, width), half)
    return pl.pallas_call(
        functools.partial(layer_kernel, shifts, nbits),
        in_specs=[HBM_SPEC] * 8,
        out_specs=[VMEM_SPEC] * 7,
        out_shape=[flat, VMEM((rows, width), F32)]
        + [VMEM((nsend, BLK, width), half)] * 3
        + [VMEM((high, width), F32), VMEM((1, width), F32)],
        scratch_shapes=[
            VMEM(cols.shape, jnp.int32),
            pltpu.SMEM(sends.shape, jnp.int32),
            VMEM(pins.shape, jnp.int32),
            VMEM((1, width), F32),
            VMEM(blocks.shape, half),
            VMEM((ntiles, BLK, BLK), half),
            VMEM((ntiles + 1, BLK, BLK), half),
            VMEM((ntiles + 1, BLK, BLK), half),
            flat,
            flat,
            VMEM((rows, LANES), F32),
            square,
            VMEM((width, width), half),
            square,
            square,
            VMEM((3, nsend * BLK, width), half),
            VMEM((ZQ, 2 * step * BLK, width), half),
            VMEM((nsend * BLK, width), half),
        ]
        + [flat] * 5
        + [
            VMEM((ZQ, 2 * step, BLK, width), half),
            VMEM((nsend, BLK, width), half),
        ]
        + [VMEM((high, width), F32)]
        + [VMEM((nbits, high // 2, width), half)] * 2
        + [
            square,
            VMEM((8, width), F32),
            VMEM((nbits, 8, width), F32),
            VMEM((nbits, 8, width), F32),
            VMEM((8, width), F32),
            VMEM((3 * nblock, LANES), jnp.int32),
            pltpu.SMEM((3 * nblock, LANES), jnp.int32),
            sem((9,)),
            sem((2, ZQ)),
            sem((2, ZQ)),
            sem,
            sem,
            sem,
            sem,
            sem((CQ,)),
            sem((CQ,)),
            sem((CQ,)),
            sem((CQ,)),
            sem((2, ZQ)),
            sem((2, ZQ)),
            sem,
            sem,
        ]
        + [sem((nbits,))] * 8,
        compiler_params=pltpu.CompilerParams(
            vmem_limit_bytes=52 << 20, collective_id=0, has_side_effects=True
        ),
        name="layer",
    )(cols, sends, pins, bias.reshape(1, width), blocks, tiles.reshape(ntiles, BLK, BLK), weight, cotan)


def join_kernel(sends_any, out_ref, acc_ref, in0_ref, in1_ref, in2_ref, dw_ref, db_ref, out, dfeat, dw, db, lines, sends_ref, inverse, sems):
    nblock = lines.shape[0]
    nsend, _, width = in0_ref.shape
    copies = [
        pltpu.make_async_copy(out_ref, out, sems.at[0]),
        pltpu.make_async_copy(dw_ref, dw, sems.at[1]),
        pltpu.make_async_copy(db_ref, db, sems.at[2]),
    ]
    get_sends = pltpu.make_async_copy(sends_any, sends_ref, sems.at[3 + nblock])
    get_sends.start()
    for copy in copies:
        copy.start()
    get_sends.wait()
    for m in range(3):
        for b in range(nblock):
            inverse[m, b] = nsend
        for j in range(nsend):
            inverse[m, sends_ref[m, 0, j]] = j

    def one_block(b, carry):
        span = pl.ds(pl.multiple_of(b * BLK, BLK), BLK)
        total = acc_ref[span, :]
        for m, ref in enumerate((in0_ref, in1_ref, in2_ref)):
            at = inverse[m, b]
            held = ref[jnp.minimum(at, nsend - 1)].astype(F32)
            total = total + held * jnp.where(at < nsend, 1.0, 0.0)
        lines[b] = total.astype(lines.dtype)
        pltpu.make_async_copy(lines.at[b], dfeat.at[b], sems.at[3 + b]).start()
        return carry

    lax.fori_loop(0, nblock, one_block, 0, unroll=2)
    for b in range(nblock):
        pltpu.make_async_copy(lines.at[b], dfeat.at[b], sems.at[3 + b]).wait()
    for copy in copies:
        copy.wait()


def join_call(sends, out, acc, in0, in1, in2, dw, db):
    rows, width = out.shape
    blocks = (rows // BLK, BLK, width)
    return pl.pallas_call(
        join_kernel,
        in_specs=[ANY_SPEC] + [VMEM_SPEC] * 7,
        out_specs=[HBM_SPEC] * 4,
        out_shape=[
            jax.ShapeDtypeStruct(out.shape, out.dtype),
            jax.ShapeDtypeStruct(blocks, out.dtype),
            jax.ShapeDtypeStruct(dw.shape, dw.dtype),
            jax.ShapeDtypeStruct(db.shape, db.dtype),
        ],
        scratch_shapes=[
            VMEM(blocks, out.dtype),
            pltpu.SMEM(sends.shape, jnp.int32),
            pltpu.SMEM((3, blocks[0]), jnp.int32),
            pltpu.SemaphoreType.DMA((4 + blocks[0],)),
        ],
        compiler_params=pltpu.CompilerParams(vmem_limit_bytes=8 << 20),
        name="join",
    )(sends, out, acc, in0, in1, in2, dw, db)


def body(feats, tiles, tile_cols, sends, pins, weight, bias, cotan):
    nbits = lax.axis_size("dom").bit_length() - 1
    shifts = (0, nbits // 2, nbits - 1)
    sends = jnp.transpose(sends, (1, 0, 2))
    results = layer_call(
        tile_cols, sends, pins, bias, feats, tiles, weight, cotan, shifts, nbits
    )
    out, dfeat, dweight, dbias = join_call(sends, *results)
    return (out, dfeat.reshape(feats.shape), dweight, dbias.reshape(-1))


def solution(mesh):
    return jax.shard_map(
        body,
        mesh=mesh,
        in_specs=(
            P(("basin", "dom"), "hid"),
            P(("basin", "dom"), None, None, None),
            P(("basin", "dom"), None),
            P(("basin", "dom"), None, None),
            P(("basin", "dom"), None),
            P(None, "hid"),
            P("hid"),
            P(("basin", "dom"), "hid"),
        ),
        out_specs=(
            P(("basin", "dom"), "hid"),
            P(("basin", "dom"), "hid"),
            P("basin", "hid"),
            P(("basin", "hid")),
        ),
        check_vma=False,
    )
```

```python
import functools
import math

import jax
import jax.numpy as jnp
from jax import lax
from jax.experimental import pallas as pl
from jax.experimental.pallas import tpu as pltpu
from jax.sharding import PartitionSpec as P

BLK = 128
LANES = 128
ZQ = 8
CQ = 4
GROUP = 4
VMEM = pltpu.VMEM
F32 = jnp.float32

MESH = pl.DeviceIdType.MESH
SMEM_SPEC = pl.BlockSpec(memory_space=pltpu.SMEM)
VMEM_SPEC = pl.BlockSpec(memory_space=pltpu.VMEM)
ANY_SPEC = pl.BlockSpec(memory_space=pl.ANY)
HBM_SPEC = pl.BlockSpec(memory_space=pltpu.HBM)
LAG = 2
FEEDS = (1, 2, 3, 1, 1)

DEEP = (((0,), (0,)), ((), ()))


def flipped(index, bit):
    return index + (1 - 2 * ((index // (1 << bit)) % 2)) * (1 << bit)


def tables(cols, sends_ref):
    nblock, ntile = cols.shape
    lane = lax.broadcasted_iota(jnp.int32, (nblock, LANES), 1)
    row = lax.broadcasted_iota(jnp.int32, (nblock, LANES), 0)
    wide = jnp.concatenate([cols, jnp.full((nblock, LANES - ntile), LANES, jnp.int32)], axis=1)
    one = [jnp.broadcast_to(cols[:, k : k + 1], (nblock, LANES)) for k in range(ntile)]
    rank = jnp.zeros((nblock, LANES), jnp.int32)
    upto = jnp.zeros((nblock, LANES), jnp.int32)
    same = jnp.zeros((nblock, LANES), jnp.int32)
    for k in range(ntile):
        before = (one[k] < wide) | ((one[k] == wide) & (k < lane))
        rank = rank + jnp.where(before, 1, 0)
        upto = upto + jnp.where(one[k] <= lane, 1, 0)
        same = same + jnp.where(one[k] == lane, 1, 0)
    merged = jnp.where(same > 0, row * ntile + upto - 1, nblock * ntile)
    perm = jnp.zeros((nblock, LANES), jnp.int32)
    here = jnp.full((nblock, LANES), -1, jnp.int32)
    prev = jnp.full((nblock, LANES), -2, jnp.int32)
    for k in range(ntile):
        at = jnp.broadcast_to(rank[:, k : k + 1], (nblock, LANES))
        perm = perm + jnp.where(at == lane, row * ntile + k, 0)
        here = jnp.where(at == lane, one[k], here)
        prev = jnp.where(at + 1 == lane, one[k], prev)
    chain = jnp.where(here == prev, 1, 0)
    lanes = lax.broadcasted_iota(jnp.int32, (8, LANES), 1)
    nsend = sends_ref.shape[2]
    inverse = jnp.full((8, LANES), nsend, jnp.int32)
    for j in range(nsend):
        inverse = jnp.where(lanes == sends_ref[0, 0, j], j, inverse)
    return jnp.concatenate([perm, chain, merged, inverse], axis=0)


def layer_kernel(
    shifts, nbits,
    cols_hbm, sends_hbm, pins_hbm, bias_hbm, feats_hbm, tiles_hbm, w_hbm, cotan_hbm,
    outv, acc, in1, in2, dwv, db_ref,
    cols_ref, sends_ref, pins_ref, bias_ref, feats, held, fold, turned, cotan, kcot, keep, w, wx, wp, wt,
    outbox, rz, r0, agg, other, dpre, dother, dagg,
    bz, b0, in0, wsum, outw, inw, gath, bsum, bout, bin_, bfin, tabv, tab,
    fetch_sem, zsend, zrecv, msend, mrecv, xsend, xrecv, asend, arecv, dsend, drecv,
    bsend, brecv, nsend_sem, nrecv_sem, rsend, rrecv, gsend, grecv, vsend, vrecv, hsend, hrecv,
):
    nblock, ntile = cols_ref.shape
    width = feats.shape[2]
    rows = nblock * BLK
    ntiles = nblock * ntile
    high = w.shape[0]
    nsend = sends_ref.shape[2]
    step = nsend // ZQ
    merged = 2 * nblock
    me = lax.axis_index("dom")
    hid = lax.axis_index("hid")
    peer = 1 - hid

    def wide(start, size):
        return pl.ds(pl.multiple_of(start, 16), size)

    here = wide(hid * width, width)
    there = wide(peer * width, width)

    def remote(src, dst, send, recv, where):
        return pltpu.make_async_remote_copy(
            src_ref=src, dst_ref=dst, send_sem=send, recv_sem=recv,
            device_id=where, device_id_type=MESH,
        )

    def mate(bit):
        return {"dom": flipped(me, bit)}

    def lane_mate(bit):
        index = me
        for low in range(1, bit + 1):
            index = flipped(index, low)
        return {"dom": index}

    get_feats = pltpu.make_async_copy(feats_hbm, feats, fetch_sem.at[0])
    get_tiles = pltpu.make_async_copy(tiles_hbm, held, fetch_sem.at[1])
    get_w = pltpu.make_async_copy(w_hbm, w, fetch_sem.at[2])
    get_cotan = pltpu.make_async_copy(cotan_hbm, cotan, fetch_sem.at[3])
    small = (
        (sends_hbm, sends_ref), (cols_hbm, cols_ref), (pins_hbm, pins_ref), (bias_hbm, bias_ref),
    )
    get_small = [
        pltpu.make_async_copy(src, dst, fetch_sem.at[5 + i]) for i, (src, dst) in enumerate(small)
    ]

    barrier = pltpu.get_barrier_semaphore()
    for bit in reversed(range(nbits)):
        pl.semaphore_signal(barrier, inc=1, device_id=mate(bit), device_id_type=MESH)
    for bit in range(2, nbits):
        pl.semaphore_signal(barrier, inc=1, device_id=lane_mate(bit), device_id_type=MESH)
    pl.semaphore_signal(barrier, inc=1, device_id={"hid": peer}, device_id_type=MESH)
    for copy in get_small:
        copy.start()
    get_feats.start()
    get_w.start()

    def zcopy(m, q):
        part = pl.ds((2 - m) * step * BLK, step * BLK)
        return remote(
            outbox.at[m, pl.ds(q * step * BLK, step * BLK)], rz.at[q, part],
            zsend.at[m - 1, q], zrecv.at[m - 1, q], mate(shifts[m]),
        )

    def mcopy():
        return remote(outbox.at[0], r0, msend, mrecv, mate(shifts[0]))

    for copy in get_small:
        copy.wait()
    get_feats.wait()
    for m in (2, 1, 0):
        for j in range(nsend):
            outbox[m, j * BLK : (j + 1) * BLK] = feats[sends_ref[m, 0, j]]
    get_w.wait()
    pl.semaphore_wait(barrier, nbits + 1 + max(nbits - 2, 0))
    for q in range(ZQ):
        zcopy(2, q).start()
        zcopy(1, q).start()
        if q == 0:
            mcopy().start()
    get_tiles.start()
    get_cotan.start()
    wcopy = remote(w.at[there], wx, xsend, xrecv, {"hid": peer})
    wcopy.start()

    tabv[...] = tables(cols_ref[...], sends_ref)
    get_tab = pltpu.make_async_copy(tabv, tab, fetch_sem.at[4])
    get_tab.start()
    in0[nsend] = jnp.zeros((BLK, width), in0.dtype)
    fold[ntiles] = jnp.zeros((BLK, BLK), fold.dtype)
    turned[ntiles] = jnp.zeros((BLK, BLK), turned.dtype)
    get_tab.wait()
    get_tiles.wait()

    def fold_row(r, carry):
        total = jnp.zeros((BLK, BLK), F32)
        for n in range(ntile):
            link = tab[nblock + r, n].astype(F32)
            total = total * link + held[tab[r, n]].astype(F32)
            value = total.astype(fold.dtype)
            fold[r * ntile + n] = value
            turned[r * ntile + n] = value.T
        return carry

    lax.fori_loop(0, nblock, fold_row, 0)

    def gathered(i, sources, group=GROUP):
        return jnp.concatenate(
            [
                jnp.concatenate([fold[tab[merged + i * group + g, s]] for s in sources], axis=1)
                for g in range(group)
            ],
            axis=0,
        )

    def span_of(i):
        return wide(i * GROUP * BLK, GROUP * BLK)

    def own_part(i, carry):
        acc[span_of(i), :] = jnp.dot(
            gathered(i, range(nblock)), feats[...].reshape(rows, width), preferred_element_type=F32
        )
        return carry

    lax.fori_loop(0, nblock // GROUP, own_part, 0)

    get_cotan.wait()
    chunk = 512

    def keep_part(i, carry):
        span = wide(i * chunk, chunk)
        ids = lax.broadcasted_iota(jnp.int32, (chunk, pins_ref.shape[1]), 0) + i * chunk
        hit = jnp.where(ids == pins_ref[...], 1.0, 0.0)
        kept = jnp.broadcast_to(1.0 - jnp.max(hit, axis=1, keepdims=True), (chunk, LANES))
        keep[span, :] = kept
        both = jnp.concatenate([kept] * (width // LANES), axis=1)
        kcot[span, :] = (cotan[span, :].astype(F32) * both).astype(kcot.dtype)
        return carry

    lax.fori_loop(0, rows // chunk, keep_part, 0)
    wp[0:width] = w[here, :]
    wp[width : 2 * width] = w[there, :]
    wt[0:width] = w[here, :].T
    wcopy.wait()
    wt[width : 2 * width] = wx[...].T

    mcopy().wait()

    def near_part(i, carry):
        acc[span_of(i), :] += jnp.dot(
            gathered(i, range(nblock, nblock + nsend)), r0[...], preferred_element_type=F32
        )
        return carry

    lax.fori_loop(0, nblock // GROUP, near_part, 0)

    def far_sources(q):
        return [nblock + m * nsend + q * step + j for m in (2, 1) for j in range(step)]

    def far_part(q, i):
        return acc[span_of(i), :] + jnp.dot(
            gathered(i, far_sources(q)), rz[q], preferred_element_type=F32
        )

    for q in range(ZQ - 1):
        zcopy(2, q).wait()
        zcopy(1, q).wait()

        def some_part(i, carry, q=q):
            acc[span_of(i), :] = far_part(q, i)
            return carry

        lax.fori_loop(0, nblock // GROUP, some_part, 0)

    part = rows // CQ
    inch = min(part, 512)
    deep_rows = rows

    def piece(c):
        return wide(c * part, part)

    def acopy(c):
        return remote(
            agg.at[piece(c)], other.at[piece(c)], asend.at[c], arecv.at[c], {"hid": peer}
        )

    def dcopy(c):
        return remote(
            dpre.at[piece(c)], dother.at[piece(c)], dsend.at[c], drecv.at[c], {"hid": peer}
        )

    zcopy(2, ZQ - 1).wait()
    zcopy(1, ZQ - 1).wait()

    def last_part(i, carry):
        final = acc[piece(i), :] + jnp.dot(
            gathered(i, far_sources(ZQ - 1), nblock // CQ), rz[ZQ - 1], preferred_element_type=F32
        )
        agg[piece(i), :] = final.astype(agg.dtype)
        acopy(i).start()
        return carry

    lax.fori_loop(0, CQ, last_part, 0)

    def middle(c, carry):
        acopy(c).wait()

        def inner(i, carry):
            span = wide(c * part + i * inch, inch)
            full = jnp.concatenate([agg[span, :], other[span, :]], axis=1)
            pre = jnp.dot(full, wp[...], preferred_element_type=F32) + bias_ref[...]
            both = jnp.concatenate([keep[span, :]] * (width // LANES), axis=1)
            sig = jax.nn.sigmoid(pre)
            gate = pre * sig
            at = pl.ds(c * (part // BLK) + i * (inch // BLK), inch // BLK)
            old = feats[at].reshape(inch, width).astype(F32)
            outv[span, :] = (old + both * gate).astype(outv.dtype)
            dpre[span, :] = (
                kcot[span, :].astype(F32) * (sig * (1.0 + pre * (1.0 - sig)))
            ).astype(dpre.dtype)
            return carry

        lax.fori_loop(0, part // inch, inner, 0)
        dcopy(c).start()
        return carry

    lax.fori_loop(0, CQ, middle, 0)

    wsum[...] = jnp.zeros_like(wsum)
    bsum[...] = jnp.zeros_like(bsum)

    def deep(c, carry):
        span = wide(c * deep_rows, deep_rows)
        grad = dpre[span, :]
        full = jnp.concatenate([agg[span, :], other[span, :]], axis=1)
        wsum[...] += lax.dot_general(full, grad, DEEP, preferred_element_type=F32)
        bsum[...] += jnp.sum(grad.astype(F32).reshape(deep_rows // 8, 8, width), axis=0)
        return carry

    lax.fori_loop(0, rows // deep_rows, deep, 0)

    half = high // 2
    last_bit = nbits - 1

    def digit(bit):
        return (me // (1 << bit)) % 2

    lower = wide(digit(0) * half, half)
    upper = wide((1 - digit(0)) * half, half)

    def differ(bit):
        return digit(bit) != digit(bit + 1)

    def taking(bit):
        on = me >= 0
        for low in range(1, bit):
            on = on & differ(low)
        return on

    def half_copies(bit):
        where = mate(0) if bit == 0 else lane_mate(bit)
        return (
            remote(outw.at[bit], inw.at[bit], rsend.at[bit], rrecv.at[bit], where),
            remote(bout.at[bit], bin_.at[bit], vsend.at[bit], vrecv.at[bit], where),
        )

    def sum_start(bit):
        def go():
            outw[bit] = wsum[upper if bit == 0 else lower].astype(outw.dtype)
            bout[bit] = bsum[...]
            for copy in half_copies(bit):
                copy.start()

        if bit == 0:
            go()
        elif bit == last_bit:
            pl.when(taking(bit))(go)
        else:
            pl.when(taking(bit) & jnp.logical_not(differ(bit)))(go)

    def sum_end(bit):
        def come():
            for copy in half_copies(bit):
                copy.wait_recv()
            if bit == last_bit:
                both = outw[bit].astype(F32) + inw[bit].astype(F32)
                gath[lower] = both.astype(gath.dtype)
                bfin[...] = bout[bit] + bin_[bit]
            else:
                wsum[lower] += inw[bit].astype(F32)
                bsum[...] += bin_[bit]

        if bit == 0:
            come()
        elif bit == last_bit:
            pl.when(taking(bit))(come)
        else:
            pl.when(taking(bit) & differ(bit))(come)

    def back_copies(bit):
        return (
            remote(gath.at[lower], gath.at[lower], gsend.at[bit], grecv.at[bit], lane_mate(bit)),
            remote(bfin, bfin, hsend.at[bit], hrecv.at[bit], lane_mate(bit)),
        )

    def side_copy():
        return remote(gath.at[lower], gath.at[lower], gsend.at[0], grecv.at[0], mate(0))

    def back_start(bit):
        if bit == 0:
            side_copy().start()
            return

        def go():
            for copy in back_copies(bit):
                copy.start()

        pl.when(taking(bit) & differ(bit))(go)

    def back_end(bit):
        if bit == 0:
            side_copy().wait()
            return

        def come():
            for copy in back_copies(bit):
                copy.wait_recv()

        pl.when(taking(bit) & jnp.logical_not(differ(bit)))(come)

    boxes = {1: in1, 2: in2}

    def bcopy(m, q):
        return remote(
            bz.at[q, pl.ds((2 - m) * step, step)], boxes[m].at[pl.ds(q * step, step)],
            bsend.at[m - 1, q], brecv.at[m - 1, q], mate(shifts[m]),
        )

    def idle(bit):
        on = taking(bit) if bit == last_bit else taking(bit) & differ(bit)
        return jnp.logical_not(on)

    paced = {}

    def pace(bit, piece_at):
        paced[piece_at] = bit

        def hold():
            bcopy(2, piece_at).wait()
            bcopy(1, piece_at).wait()

        pl.when(idle(bit))(hold)

    def drain():
        for bit in range(nbits):
            def sent(bit=bit):
                for copy in half_copies(bit):
                    copy.wait_send()

            if bit == 0:
                sent()
            elif bit == last_bit:
                pl.when(taking(bit))(sent)
            else:
                pl.when(taking(bit) & jnp.logical_not(differ(bit)))(sent)
        for bit in range(1, last_bit):
            def given(bit=bit):
                for copy in back_copies(bit):
                    copy.wait_send()

            pl.when(taking(bit) & differ(bit))(given)

    stages = [(sum_start, sum_end, bit) for bit in range(nbits)]
    stages += [(back_start, back_end, bit) for bit in reversed(range(last_bit))]

    stages[0][0](stages[0][2])

    def undo(c, carry):
        dcopy(2 * c).wait()
        dcopy(2 * c + 1).wait()
        span = wide(c * 2 * part, 2 * part)
        both = jnp.concatenate([dpre[span, :], dother[span, :]], axis=1)
        dagg[span, :] = jnp.dot(both, wt[...], preferred_element_type=F32).astype(dagg.dtype)
        return carry

    lax.fori_loop(0, CQ // 2, undo, 0)

    def spread(sources):
        lhs = jnp.concatenate(
            [
                jnp.concatenate([turned[tab[merged + r, s]] for r in range(nblock)], axis=1)
                for s in sources
            ],
            axis=0,
        )
        return jnp.dot(lhs, dagg[...], preferred_element_type=F32)

    def far_back(q, carry):
        bz[q] = spread(far_sources(q)).astype(bz.dtype).reshape(2 * step, BLK, width)
        bcopy(2, q).start()
        bcopy(1, q).start()
        return carry

    def near_back(i, carry):
        sources = [nblock + i * GROUP + g for g in range(GROUP)]
        b0[pl.ds(i * GROUP, GROUP)] = spread(sources).astype(b0.dtype).reshape(GROUP, BLK, width)
        return carry

    lax.fori_loop(0, nsend // GROUP, near_back, 0)
    ncopy = remote(b0, in0.at[pl.ds(0, nsend)], nsend_sem, nrecv_sem, mate(shifts[0]))

    def own_back(i, carry):
        span = span_of(i)
        acc[span, :] = cotan[span, :].astype(F32) + spread([i * GROUP + g for g in range(GROUP)])
        return carry

    def add_near(b, carry):
        acc[wide(b * BLK, BLK), :] += in0[tab[3 * nblock, b]].astype(F32)
        return carry

    def feed(stage, fed):
        count = FEEDS[stage] if stage < len(FEEDS) else 0
        lax.fori_loop(fed, fed + count, far_back, 0)
        return fed + count

    fed = feed(0, 0)
    lax.fori_loop(0, nsend // GROUP, near_back, 0)
    groups = nblock // GROUP
    for i in range(len(stages)):
        stages[i][1](stages[i][2])
        if 0 < i < nbits and LAG <= fed < ZQ and fed - LAG not in paced:
            pace(i, fed - LAG)
        if i + 1 < len(stages):
            stages[i + 1][0](stages[i + 1][2])
            fed = feed(i + 1, fed)
        if i == 0:
            ncopy.start()
        if i < 2:
            lax.fori_loop(i * groups // 2, (i + 1) * groups // 2, own_back, 0)
        if i == len(stages) - 2:
            ncopy.wait()
            lax.fori_loop(0, nblock, add_near, 0)
    scale = 1.0 / math.sqrt((1 << nbits) * rows)
    dwv[here] = gath[0:width].astype(F32) * scale
    dwv[there] = gath[width : 2 * width].astype(F32) * scale
    db_ref[...] = jnp.sum(bfin[...], axis=0, keepdims=True) * scale
    drain()

    for q in range(ZQ):
        def landed(q=q):
            bcopy(2, q).wait()
            bcopy(1, q).wait()

        if q in paced:
            pl.when(jnp.logical_not(idle(paced[q])))(landed)
        else:
            landed()


def layer_call(cols, sends, pins, bias, feats, tiles, weight, cotan, shifts, nbits):
    rows, width = feats.shape
    nblock, ntile = cols.shape
    ntiles = nblock * ntile
    high = weight.shape[0]
    nsend = sends.shape[2]
    step = nsend // ZQ
    blocks = feats.reshape(nblock, BLK, width)
    sem = pltpu.SemaphoreType.DMA
    half = feats.dtype
    flat = VMEM((rows, width), half)
    square = VMEM((high, width), half)
    return pl.pallas_call(
        functools.partial(layer_kernel, shifts, nbits),
        in_specs=[HBM_SPEC] * 8,
        out_specs=[VMEM_SPEC] * 6,
        out_shape=[flat, VMEM((rows, width), F32)]
        + [VMEM((nsend, BLK, width), half)] * 2
        + [VMEM((high, width), F32), VMEM((1, width), F32)],
        scratch_shapes=[
            VMEM(cols.shape, jnp.int32),
            pltpu.SMEM(sends.shape, jnp.int32),
            VMEM(pins.shape, jnp.int32),
            VMEM((1, width), F32),
            VMEM(blocks.shape, half),
            VMEM((ntiles, BLK, BLK), half),
            VMEM((ntiles + 1, BLK, BLK), half),
            VMEM((ntiles + 1, BLK, BLK), half),
            flat,
            flat,
            VMEM((rows, LANES), F32),
            square,
            VMEM((width, width), half),
            square,
            square,
            VMEM((3, nsend * BLK, width), half),
            VMEM((ZQ, 2 * step * BLK, width), half),
            VMEM((nsend * BLK, width), half),
        ]
        + [flat] * 5
        + [
            VMEM((ZQ, 2 * step, BLK, width), half),
            VMEM((nsend, BLK, width), half),
            VMEM((nsend + 1, BLK, width), half),
        ]
        + [VMEM((high, width), F32)]
        + [VMEM((nbits, high // 2, width), half)] * 2
        + [
            square,
            VMEM((8, width), F32),
            VMEM((nbits, 8, width), F32),
            VMEM((nbits, 8, width), F32),
            VMEM((8, width), F32),
            VMEM((3 * nblock + 8, LANES), jnp.int32),
            pltpu.SMEM((3 * nblock + 8, LANES), jnp.int32),
            sem((9,)),
            sem((2, ZQ)),
            sem((2, ZQ)),
            sem,
            sem,
            sem,
            sem,
            sem((CQ,)),
            sem((CQ,)),
            sem((CQ,)),
            sem((CQ,)),
            sem((2, ZQ)),
            sem((2, ZQ)),
            sem,
            sem,
        ]
        + [sem((nbits,))] * 8,
        compiler_params=pltpu.CompilerParams(
            vmem_limit_bytes=52 << 20, collective_id=0, has_side_effects=True
        ),
        name="layer",
    )(cols, sends, pins, bias.reshape(1, width), blocks, tiles.reshape(ntiles, BLK, BLK), weight, cotan)


def join_kernel(sends_any, out_ref, acc_ref, in1_ref, in2_ref, dw_ref, db_ref, out, dfeat, dw, db, lines, sends_ref, inverse, sems):
    nblock = lines.shape[0]
    nsend, _, width = in1_ref.shape
    copies = [
        pltpu.make_async_copy(out_ref, out, sems.at[0]),
        pltpu.make_async_copy(dw_ref, dw, sems.at[1]),
        pltpu.make_async_copy(db_ref, db, sems.at[2]),
    ]
    get_sends = pltpu.make_async_copy(sends_any, sends_ref, sems.at[3 + nblock])
    get_sends.start()
    for copy in copies:
        copy.start()
    get_sends.wait()
    for m in (1, 2):
        for b in range(nblock):
            inverse[m, b] = nsend
        for j in range(nsend):
            inverse[m, sends_ref[m, 0, j]] = j

    def one_block(b, carry):
        span = pl.ds(pl.multiple_of(b * BLK, BLK), BLK)
        total = acc_ref[span, :]
        for m, ref in ((1, in1_ref), (2, in2_ref)):
            at = inverse[m, b]
            held = ref[jnp.minimum(at, nsend - 1)].astype(F32)
            total = total + held * jnp.where(at < nsend, 1.0, 0.0)
        lines[b] = total.astype(lines.dtype)
        pltpu.make_async_copy(lines.at[b], dfeat.at[b], sems.at[3 + b]).start()
        return carry

    lax.fori_loop(0, nblock, one_block, 0, unroll=2)
    for b in range(nblock):
        pltpu.make_async_copy(lines.at[b], dfeat.at[b], sems.at[3 + b]).wait()
    for copy in copies:
        copy.wait()


def join_call(sends, out, acc, in1, in2, dw, db):
    rows, width = out.shape
    blocks = (rows // BLK, BLK, width)
    return pl.pallas_call(
        join_kernel,
        in_specs=[ANY_SPEC] + [VMEM_SPEC] * 6,
        out_specs=[HBM_SPEC] * 4,
        out_shape=[
            jax.ShapeDtypeStruct(out.shape, out.dtype),
            jax.ShapeDtypeStruct(blocks, out.dtype),
            jax.ShapeDtypeStruct(dw.shape, dw.dtype),
            jax.ShapeDtypeStruct(db.shape, db.dtype),
        ],
        scratch_shapes=[
            VMEM(blocks, out.dtype),
            pltpu.SMEM(sends.shape, jnp.int32),
            pltpu.SMEM((3, blocks[0]), jnp.int32),
            pltpu.SemaphoreType.DMA((4 + blocks[0],)),
        ],
        compiler_params=pltpu.CompilerParams(vmem_limit_bytes=8 << 20),
        name="join",
    )(sends, out, acc, in1, in2, dw, db)


def body(feats, tiles, tile_cols, sends, pins, weight, bias, cotan):
    nbits = lax.axis_size("dom").bit_length() - 1
    shifts = (0, nbits // 2, nbits - 1)
    sends = jnp.transpose(sends, (1, 0, 2))
    results = layer_call(
        tile_cols, sends, pins, bias, feats, tiles, weight, cotan, shifts, nbits
    )
    out, dfeat, dweight, dbias = join_call(sends, *results)
    return (out, dfeat.reshape(feats.shape), dweight, dbias.reshape(-1))


def solution(mesh):
    return jax.shard_map(
        body,
        mesh=mesh,
        in_specs=(
            P(("basin", "dom"), "hid"),
            P(("basin", "dom"), None, None, None),
            P(("basin", "dom"), None),
            P(("basin", "dom"), None, None),
            P(("basin", "dom"), None),
            P(None, "hid"),
            P("hid"),
            P(("basin", "dom"), "hid"),
        ),
        out_specs=(
            P(("basin", "dom"), "hid"),
            P(("basin", "dom"), "hid"),
            P("basin", "hid"),
            P(("basin", "hid")),
        ),
        check_vma=False,
    )
```

```python
import functools
import math

import jax
import jax.numpy as jnp
from jax import lax
from jax.experimental import pallas as pl
from jax.experimental.pallas import tpu as pltpu
from jax.sharding import PartitionSpec as P

BLK = 128
LANES = 128
ZQ = 8
CQ = 4
GROUP = 4
VMEM = pltpu.VMEM
F32 = jnp.float32

MESH = pl.DeviceIdType.MESH
SMEM_SPEC = pl.BlockSpec(memory_space=pltpu.SMEM)
VMEM_SPEC = pl.BlockSpec(memory_space=pltpu.VMEM)
ANY_SPEC = pl.BlockSpec(memory_space=pl.ANY)
HBM_SPEC = pl.BlockSpec(memory_space=pltpu.HBM)
LAG = 2
FEEDS = (1, 2, 3, 1, 1)

DEEP = (((0,), (0,)), ((), ()))


def flipped(index, bit):
    return index + (1 - 2 * ((index // (1 << bit)) % 2)) * (1 << bit)


def tables(cols, sends_ref):
    nblock, ntile = cols.shape
    lane = lax.broadcasted_iota(jnp.int32, (nblock, LANES), 1)
    row = lax.broadcasted_iota(jnp.int32, (nblock, LANES), 0)
    wide = jnp.concatenate([cols, jnp.full((nblock, LANES - ntile), LANES, jnp.int32)], axis=1)
    one = [jnp.broadcast_to(cols[:, k : k + 1], (nblock, LANES)) for k in range(ntile)]
    rank = jnp.zeros((nblock, LANES), jnp.int32)
    upto = jnp.zeros((nblock, LANES), jnp.int32)
    same = jnp.zeros((nblock, LANES), jnp.int32)
    for k in range(ntile):
        before = (one[k] < wide) | ((one[k] == wide) & (k < lane))
        rank = rank + jnp.where(before, 1, 0)
        upto = upto + jnp.where(one[k] <= lane, 1, 0)
        same = same + jnp.where(one[k] == lane, 1, 0)
    merged = jnp.where(same > 0, row * ntile + upto - 1, nblock * ntile)
    perm = jnp.zeros((nblock, LANES), jnp.int32)
    here = jnp.full((nblock, LANES), -1, jnp.int32)
    prev = jnp.full((nblock, LANES), -2, jnp.int32)
    for k in range(ntile):
        at = jnp.broadcast_to(rank[:, k : k + 1], (nblock, LANES))
        perm = perm + jnp.where(at == lane, row * ntile + k, 0)
        here = jnp.where(at == lane, one[k], here)
        prev = jnp.where(at + 1 == lane, one[k], prev)
    chain = jnp.where(here == prev, 1, 0)
    lanes = lax.broadcasted_iota(jnp.int32, (8, LANES), 1)
    nsend = sends_ref.shape[2]
    inverse = jnp.full((8, LANES), nsend, jnp.int32)
    for j in range(nsend):
        inverse = jnp.where(lanes == sends_ref[0, 0, j], j, inverse)
    return jnp.concatenate([perm, chain, merged, inverse], axis=0)


def layer_kernel(
    shifts, nbits,
    cols_hbm, sends_hbm, pins_hbm, bias_hbm, feats_hbm, tiles_hbm, w_hbm, cotan_hbm,
    outv, acc, in1, in2, dwv, db_ref,
    cols_ref, sends_ref, pins_ref, bias_ref, feats, held, fold, turned, cotan, kcot, keep, w, wx, wp, wt,
    outbox, rz, r0, agg, other, dpre, dother, dagg,
    bz, b0, in0, wsum, outw, inw, gath, bsum, bout, bin_, bfin, tabv, tab,
    fetch_sem, zsend, zrecv, msend, mrecv, xsend, xrecv, asend, arecv, dsend, drecv,
    bsend, brecv, nsend_sem, nrecv_sem, rsend, rrecv, gsend, grecv, vsend, vrecv, hsend, hrecv,
):
    nblock, ntile = cols_ref.shape
    width = feats.shape[2]
    rows = nblock * BLK
    ntiles = nblock * ntile
    high = w.shape[0]
    nsend = sends_ref.shape[2]
    step = nsend // ZQ
    merged = 2 * nblock
    me = lax.axis_index("dom")
    hid = lax.axis_index("hid")
    peer = 1 - hid

    def wide(start, size):
        return pl.ds(pl.multiple_of(start, 16), size)

    here = wide(hid * width, width)
    there = wide(peer * width, width)

    def remote(src, dst, send, recv, where):
        return pltpu.make_async_remote_copy(
            src_ref=src, dst_ref=dst, send_sem=send, recv_sem=recv,
            device_id=where, device_id_type=MESH,
        )

    def mate(bit):
        return {"dom": flipped(me, bit)}

    def lane_mate(bit):
        index = me
        for low in range(1, bit + 1):
            index = flipped(index, low)
        return {"dom": index}

    get_feats = pltpu.make_async_copy(feats_hbm, feats, fetch_sem.at[0])
    get_tiles = pltpu.make_async_copy(tiles_hbm, held, fetch_sem.at[1])
    get_w = pltpu.make_async_copy(w_hbm, w, fetch_sem.at[2])
    get_cotan = pltpu.make_async_copy(cotan_hbm, cotan, fetch_sem.at[3])
    small = (
        (sends_hbm, sends_ref), (cols_hbm, cols_ref), (pins_hbm, pins_ref), (bias_hbm, bias_ref),
    )
    get_small = [
        pltpu.make_async_copy(src, dst, fetch_sem.at[5 + i]) for i, (src, dst) in enumerate(small)
    ]

    barrier = pltpu.get_barrier_semaphore()
    for bit in reversed(range(nbits)):
        pl.semaphore_signal(barrier, inc=1, device_id=mate(bit), device_id_type=MESH)
    for bit in range(2, nbits):
        pl.semaphore_signal(barrier, inc=1, device_id=lane_mate(bit), device_id_type=MESH)
    pl.semaphore_signal(barrier, inc=1, device_id={"hid": peer}, device_id_type=MESH)
    for copy in get_small:
        copy.start()
    get_feats.start()
    get_w.start()

    def zcopy(m, q):
        part = pl.ds((2 - m) * step * BLK, step * BLK)
        return remote(
            outbox.at[m, pl.ds(q * step * BLK, step * BLK)], rz.at[q, part],
            zsend.at[m - 1, q], zrecv.at[m - 1, q], mate(shifts[m]),
        )

    def mcopy():
        return remote(outbox.at[0], r0, msend, mrecv, mate(shifts[0]))

    for copy in get_small:
        copy.wait()
    get_feats.wait()
    for m in (2, 1, 0):
        for j in range(nsend):
            outbox[m, j * BLK : (j + 1) * BLK] = feats[sends_ref[m, 0, j]]
    get_w.wait()
    pl.semaphore_wait(barrier, nbits + 1 + max(nbits - 2, 0))
    for q in range(ZQ):
        zcopy(2, q).start()
        zcopy(1, q).start()
        if q == 2:
            mcopy().start()
    get_tiles.start()
    get_cotan.start()
    wcopy = remote(w.at[there], wx, xsend, xrecv, {"hid": peer})
    wcopy.start()

    tabv[...] = tables(cols_ref[...], sends_ref)
    get_tab = pltpu.make_async_copy(tabv, tab, fetch_sem.at[4])
    get_tab.start()
    in0[nsend] = jnp.zeros((BLK, width), in0.dtype)
    fold[ntiles] = jnp.zeros((BLK, BLK), fold.dtype)
    turned[ntiles] = jnp.zeros((BLK, BLK), turned.dtype)
    get_tab.wait()
    get_tiles.wait()

    def fold_row(r, carry):
        total = jnp.zeros((BLK, BLK), F32)
        for n in range(ntile):
            link = tab[nblock + r, n].astype(F32)
            total = total * link + held[tab[r, n]].astype(F32)
            value = total.astype(fold.dtype)
            fold[r * ntile + n] = value
            turned[r * ntile + n] = value.T
        return carry

    lax.fori_loop(0, nblock, fold_row, 0)

    def gathered(i, sources, group=GROUP):
        return jnp.concatenate(
            [
                jnp.concatenate([fold[tab[merged + i * group + g, s]] for s in sources], axis=1)
                for g in range(group)
            ],
            axis=0,
        )

    def span_of(i):
        return wide(i * GROUP * BLK, GROUP * BLK)

    def own_part(i, carry):
        acc[span_of(i), :] = jnp.dot(
            gathered(i, range(nblock)), feats[...].reshape(rows, width), preferred_element_type=F32
        )
        return carry

    lax.fori_loop(0, nblock // GROUP, own_part, 0)

    get_cotan.wait()
    chunk = 512

    def keep_part(i, carry):
        span = wide(i * chunk, chunk)
        ids = lax.broadcasted_iota(jnp.int32, (chunk, pins_ref.shape[1]), 0) + i * chunk
        hit = jnp.where(ids == pins_ref[...], 1.0, 0.0)
        kept = jnp.broadcast_to(1.0 - jnp.max(hit, axis=1, keepdims=True), (chunk, LANES))
        keep[span, :] = kept
        both = jnp.concatenate([kept] * (width // LANES), axis=1)
        kcot[span, :] = (cotan[span, :].astype(F32) * both).astype(kcot.dtype)
        return carry

    lax.fori_loop(0, rows // chunk, keep_part, 0)
    wp[0:width] = w[here, :]
    wp[width : 2 * width] = w[there, :]
    wt[0:width] = w[here, :].T
    wcopy.wait()
    wt[width : 2 * width] = wx[...].T

    mcopy().wait()

    def near_part(i, carry):
        acc[span_of(i), :] += jnp.dot(
            gathered(i, range(nblock, nblock + nsend)), r0[...], preferred_element_type=F32
        )
        return carry

    lax.fori_loop(0, nblock // GROUP, near_part, 0)

    def far_sources(q):
        return [nblock + m * nsend + q * step + j for m in (2, 1) for j in range(step)]

    def far_part(q, i):
        return acc[span_of(i), :] + jnp.dot(
            gathered(i, far_sources(q)), rz[q], preferred_element_type=F32
        )

    for q in range(ZQ - 1):
        zcopy(2, q).wait()
        zcopy(1, q).wait()

        def some_part(i, carry, q=q):
            acc[span_of(i), :] = far_part(q, i)
            return carry

        lax.fori_loop(0, nblock // GROUP, some_part, 0)

    part = rows // CQ
    inch = min(part, 512)
    deep_rows = rows

    def piece(c):
        return wide(c * part, part)

    def acopy(c):
        return remote(
            agg.at[piece(c)], other.at[piece(c)], asend.at[c], arecv.at[c], {"hid": peer}
        )

    def dcopy(c):
        return remote(
            dpre.at[piece(c)], dother.at[piece(c)], dsend.at[c], drecv.at[c], {"hid": peer}
        )

    zcopy(2, ZQ - 1).wait()
    zcopy(1, ZQ - 1).wait()

    def last_part(i, carry):
        final = acc[piece(i), :] + jnp.dot(
            gathered(i, far_sources(ZQ - 1), nblock // CQ), rz[ZQ - 1], preferred_element_type=F32
        )
        agg[piece(i), :] = final.astype(agg.dtype)
        acopy(i).start()
        return carry

    lax.fori_loop(0, CQ, last_part, 0)

    def middle(c, carry):
        acopy(c).wait()

        def inner(i, carry):
            span = wide(c * part + i * inch, inch)
            full = jnp.concatenate([agg[span, :], other[span, :]], axis=1)
            pre = jnp.dot(full, wp[...], preferred_element_type=F32) + bias_ref[...]
            both = jnp.concatenate([keep[span, :]] * (width // LANES), axis=1)
            sig = jax.nn.sigmoid(pre)
            gate = pre * sig
            at = pl.ds(c * (part // BLK) + i * (inch // BLK), inch // BLK)
            old = feats[at].reshape(inch, width).astype(F32)
            outv[span, :] = (old + both * gate).astype(outv.dtype)
            dpre[span, :] = (
                kcot[span, :].astype(F32) * (sig * (1.0 + pre * (1.0 - sig)))
            ).astype(dpre.dtype)
            return carry

        lax.fori_loop(0, part // inch, inner, 0)
        dcopy(c).start()
        return carry

    lax.fori_loop(0, CQ, middle, 0)

    wsum[...] = jnp.zeros_like(wsum)
    bsum[...] = jnp.zeros_like(bsum)

    def deep(c, carry):
        span = wide(c * deep_rows, deep_rows)
        grad = dpre[span, :]
        full = jnp.concatenate([agg[span, :], other[span, :]], axis=1)
        wsum[...] += lax.dot_general(full, grad, DEEP, preferred_element_type=F32)
        bsum[...] += jnp.sum(grad.astype(F32).reshape(deep_rows // 8, 8, width), axis=0)
        return carry

    lax.fori_loop(0, rows // deep_rows, deep, 0)

    half = high // 2
    last_bit = nbits - 1

    def digit(bit):
        return (me // (1 << bit)) % 2

    lower = wide(digit(0) * half, half)
    upper = wide((1 - digit(0)) * half, half)

    def differ(bit):
        return digit(bit) != digit(bit + 1)

    def taking(bit):
        on = me >= 0
        for low in range(1, bit):
            on = on & differ(low)
        return on

    def half_copies(bit):
        where = mate(0) if bit == 0 else lane_mate(bit)
        return (
            remote(outw.at[bit], inw.at[bit], rsend.at[bit], rrecv.at[bit], where),
            remote(bout.at[bit], bin_.at[bit], vsend.at[bit], vrecv.at[bit], where),
        )

    def sum_start(bit):
        def go():
            outw[bit] = wsum[upper if bit == 0 else lower].astype(outw.dtype)
            bout[bit] = bsum[...]
            for copy in half_copies(bit):
                copy.start()

        if bit == 0:
            go()
        elif bit == last_bit:
            pl.when(taking(bit))(go)
        else:
            pl.when(taking(bit) & jnp.logical_not(differ(bit)))(go)

    def sum_end(bit):
        def come():
            for copy in half_copies(bit):
                copy.wait_recv()
            if bit == last_bit:
                both = outw[bit].astype(F32) + inw[bit].astype(F32)
                gath[lower] = both.astype(gath.dtype)
                bfin[...] = bout[bit] + bin_[bit]
            else:
                wsum[lower] += inw[bit].astype(F32)
                bsum[...] += bin_[bit]

        if bit == 0:
            come()
        elif bit == last_bit:
            pl.when(taking(bit))(come)
        else:
            pl.when(taking(bit) & differ(bit))(come)

    def back_copies(bit):
        return (
            remote(gath.at[lower], gath.at[lower], gsend.at[bit], grecv.at[bit], lane_mate(bit)),
            remote(bfin, bfin, hsend.at[bit], hrecv.at[bit], lane_mate(bit)),
        )

    def side_copy():
        return remote(gath.at[lower], gath.at[lower], gsend.at[0], grecv.at[0], mate(0))

    def back_start(bit):
        if bit == 0:
            side_copy().start()
            return

        def go():
            for copy in back_copies(bit):
                copy.start()

        pl.when(taking(bit) & differ(bit))(go)

    def back_end(bit):
        if bit == 0:
            side_copy().wait()
            return

        def come():
            for copy in back_copies(bit):
                copy.wait_recv()

        pl.when(taking(bit) & jnp.logical_not(differ(bit)))(come)

    boxes = {1: in1, 2: in2}

    def bcopy(m, q):
        return remote(
            bz.at[q, pl.ds((2 - m) * step, step)], boxes[m].at[pl.ds(q * step, step)],
            bsend.at[m - 1, q], brecv.at[m - 1, q], mate(shifts[m]),
        )

    def idle(bit):
        on = taking(bit) if bit == last_bit else taking(bit) & differ(bit)
        return jnp.logical_not(on)

    paced = {}

    def pace(bit, piece_at):
        paced[piece_at] = bit

        def hold():
            bcopy(2, piece_at).wait()
            bcopy(1, piece_at).wait()

        pl.when(idle(bit))(hold)

    def drain():
        for bit in range(nbits):
            def sent(bit=bit):
                for copy in half_copies(bit):
                    copy.wait_send()

            if bit == 0:
                sent()
            elif bit == last_bit:
                pl.when(taking(bit))(sent)
            else:
                pl.when(taking(bit) & jnp.logical_not(differ(bit)))(sent)
        for bit in range(1, last_bit):
            def given(bit=bit):
                for copy in back_copies(bit):
                    copy.wait_send()

            pl.when(taking(bit) & differ(bit))(given)

    stages = [(sum_start, sum_end, bit) for bit in range(nbits)]
    stages += [(back_start, back_end, bit) for bit in reversed(range(last_bit))]

    stages[0][0](stages[0][2])

    def undo(c, carry):
        dcopy(2 * c).wait()
        dcopy(2 * c + 1).wait()
        span = wide(c * 2 * part, 2 * part)
        both = jnp.concatenate([dpre[span, :], dother[span, :]], axis=1)
        dagg[span, :] = jnp.dot(both, wt[...], preferred_element_type=F32).astype(dagg.dtype)
        return carry

    lax.fori_loop(0, CQ // 2, undo, 0)

    def spread(sources):
        lhs = jnp.concatenate(
            [
                jnp.concatenate([turned[tab[merged + r, s]] for r in range(nblock)], axis=1)
                for s in sources
            ],
            axis=0,
        )
        return jnp.dot(lhs, dagg[...], preferred_element_type=F32)

    def far_back(q, carry):
        bz[q] = spread(far_sources(q)).astype(bz.dtype).reshape(2 * step, BLK, width)
        bcopy(2, q).start()
        bcopy(1, q).start()
        return carry

    def near_back(i, carry):
        sources = [nblock + i * GROUP + g for g in range(GROUP)]
        b0[pl.ds(i * GROUP, GROUP)] = spread(sources).astype(b0.dtype).reshape(GROUP, BLK, width)
        return carry

    lax.fori_loop(0, nsend // GROUP, near_back, 0)
    ncopy = remote(b0, in0.at[pl.ds(0, nsend)], nsend_sem, nrecv_sem, mate(shifts[0]))

    def own_back(i, carry):
        span = span_of(i)
        acc[span, :] = cotan[span, :].astype(F32) + spread([i * GROUP + g for g in range(GROUP)])
        return carry

    def add_near(b, carry):
        acc[wide(b * BLK, BLK), :] += in0[tab[3 * nblock, b]].astype(F32)
        return carry

    def feed(stage, fed):
        count = FEEDS[stage] if stage < len(FEEDS) else 0
        lax.fori_loop(fed, fed + count, far_back, 0)
        return fed + count

    fed = feed(0, 0)
    lax.fori_loop(0, nsend // GROUP, near_back, 0)
    groups = nblock // GROUP
    for i in range(len(stages)):
        stages[i][1](stages[i][2])
        if 0 < i < nbits and LAG <= fed < ZQ and fed - LAG not in paced:
            pace(i, fed - LAG)
        if i + 1 < len(stages):
            stages[i + 1][0](stages[i + 1][2])
            fed = feed(i + 1, fed)
        if i == 0:
            ncopy.start()
        if i < 2:
            lax.fori_loop(i * groups // 2, (i + 1) * groups // 2, own_back, 0)
        if i == len(stages) - 2:
            ncopy.wait()
            lax.fori_loop(0, nblock, add_near, 0)
    scale = 1.0 / math.sqrt((1 << nbits) * rows)
    dwv[here] = gath[0:width].astype(F32) * scale
    dwv[there] = gath[width : 2 * width].astype(F32) * scale
    db_ref[...] = jnp.sum(bfin[...], axis=0, keepdims=True) * scale
    drain()

    for q in range(ZQ):
        def landed(q=q):
            bcopy(2, q).wait()
            bcopy(1, q).wait()

        if q in paced:
            pl.when(jnp.logical_not(idle(paced[q])))(landed)
        else:
            landed()


def layer_call(cols, sends, pins, bias, feats, tiles, weight, cotan, shifts, nbits):
    rows, width = feats.shape
    nblock, ntile = cols.shape
    ntiles = nblock * ntile
    high = weight.shape[0]
    nsend = sends.shape[2]
    step = nsend // ZQ
    blocks = feats.reshape(nblock, BLK, width)
    sem = pltpu.SemaphoreType.DMA
    half = feats.dtype
    flat = VMEM((rows, width), half)
    square = VMEM((high, width), half)
    return pl.pallas_call(
        functools.partial(layer_kernel, shifts, nbits),
        in_specs=[HBM_SPEC] * 8,
        out_specs=[VMEM_SPEC] * 6,
        out_shape=[flat, VMEM((rows, width), F32)]
        + [VMEM((nsend, BLK, width), half)] * 2
        + [VMEM((high, width), F32), VMEM((1, width), F32)],
        scratch_shapes=[
            VMEM(cols.shape, jnp.int32),
            pltpu.SMEM(sends.shape, jnp.int32),
            VMEM(pins.shape, jnp.int32),
            VMEM((1, width), F32),
            VMEM(blocks.shape, half),
            VMEM((ntiles, BLK, BLK), half),
            VMEM((ntiles + 1, BLK, BLK), half),
            VMEM((ntiles + 1, BLK, BLK), half),
            flat,
            flat,
            VMEM((rows, LANES), F32),
            square,
            VMEM((width, width), half),
            square,
            square,
            VMEM((3, nsend * BLK, width), half),
            VMEM((ZQ, 2 * step * BLK, width), half),
            VMEM((nsend * BLK, width), half),
        ]
        + [flat] * 5
        + [
            VMEM((ZQ, 2 * step, BLK, width), half),
            VMEM((nsend, BLK, width), half),
            VMEM((nsend + 1, BLK, width), half),
        ]
        + [VMEM((high, width), F32)]
        + [VMEM((nbits, high // 2, width), half)] * 2
        + [
            square,
            VMEM((8, width), F32),
            VMEM((nbits, 8, width), F32),
            VMEM((nbits, 8, width), F32),
            VMEM((8, width), F32),
            VMEM((3 * nblock + 8, LANES), jnp.int32),
            pltpu.SMEM((3 * nblock + 8, LANES), jnp.int32),
            sem((9,)),
            sem((2, ZQ)),
            sem((2, ZQ)),
            sem,
            sem,
            sem,
            sem,
            sem((CQ,)),
            sem((CQ,)),
            sem((CQ,)),
            sem((CQ,)),
            sem((2, ZQ)),
            sem((2, ZQ)),
            sem,
            sem,
        ]
        + [sem((nbits,))] * 8,
        compiler_params=pltpu.CompilerParams(
            vmem_limit_bytes=52 << 20, collective_id=0, has_side_effects=True
        ),
        name="layer",
    )(cols, sends, pins, bias.reshape(1, width), blocks, tiles.reshape(ntiles, BLK, BLK), weight, cotan)


def join_kernel(sends_any, out_ref, acc_ref, in1_ref, in2_ref, dw_ref, db_ref, out, dfeat, dw, db, lines, sends_ref, inverse, sems):
    nblock = lines.shape[0]
    nsend, _, width = in1_ref.shape
    copies = [
        pltpu.make_async_copy(out_ref, out, sems.at[0]),
        pltpu.make_async_copy(dw_ref, dw, sems.at[1]),
        pltpu.make_async_copy(db_ref, db, sems.at[2]),
    ]
    get_sends = pltpu.make_async_copy(sends_any, sends_ref, sems.at[3 + nblock])
    get_sends.start()
    for copy in copies:
        copy.start()
    get_sends.wait()
    for m in (1, 2):
        for b in range(nblock):
            inverse[m, b] = nsend
        for j in range(nsend):
            inverse[m, sends_ref[m, 0, j]] = j

    def one_block(b, carry):
        span = pl.ds(pl.multiple_of(b * BLK, BLK), BLK)
        total = acc_ref[span, :]
        for m, ref in ((1, in1_ref), (2, in2_ref)):
            at = inverse[m, b]
            held = ref[jnp.minimum(at, nsend - 1)].astype(F32)
            total = total + held * jnp.where(at < nsend, 1.0, 0.0)
        lines[b] = total.astype(lines.dtype)
        pltpu.make_async_copy(lines.at[b], dfeat.at[b], sems.at[3 + b]).start()
        return carry

    lax.fori_loop(0, nblock, one_block, 0, unroll=2)
    for b in range(nblock):
        pltpu.make_async_copy(lines.at[b], dfeat.at[b], sems.at[3 + b]).wait()
    for copy in copies:
        copy.wait()


def join_call(sends, out, acc, in1, in2, dw, db):
    rows, width = out.shape
    blocks = (rows // BLK, BLK, width)
    return pl.pallas_call(
        join_kernel,
        in_specs=[ANY_SPEC] + [VMEM_SPEC] * 6,
        out_specs=[HBM_SPEC] * 4,
        out_shape=[
            jax.ShapeDtypeStruct(out.shape, out.dtype),
            jax.ShapeDtypeStruct(blocks, out.dtype),
            jax.ShapeDtypeStruct(dw.shape, dw.dtype),
            jax.ShapeDtypeStruct(db.shape, db.dtype),
        ],
        scratch_shapes=[
            VMEM(blocks, out.dtype),
            pltpu.SMEM(sends.shape, jnp.int32),
            pltpu.SMEM((3, blocks[0]), jnp.int32),
            pltpu.SemaphoreType.DMA((4 + blocks[0],)),
        ],
        compiler_params=pltpu.CompilerParams(vmem_limit_bytes=8 << 20),
        name="join",
    )(sends, out, acc, in1, in2, dw, db)


def body(feats, tiles, tile_cols, sends, pins, weight, bias, cotan):
    nbits = lax.axis_size("dom").bit_length() - 1
    shifts = (0, nbits // 2, nbits - 1)
    sends = jnp.transpose(sends, (1, 0, 2))
    results = layer_call(
        tile_cols, sends, pins, bias, feats, tiles, weight, cotan, shifts, nbits
    )
    out, dfeat, dweight, dbias = join_call(sends, *results)
    return (out, dfeat.reshape(feats.shape), dweight, dbias.reshape(-1))


def solution(mesh):
    return jax.shard_map(
        body,
        mesh=mesh,
        in_specs=(
            P(("basin", "dom"), "hid"),
            P(("basin", "dom"), None, None, None),
            P(("basin", "dom"), None),
            P(("basin", "dom"), None, None),
            P(("basin", "dom"), None),
            P(None, "hid"),
            P("hid"),
            P(("basin", "dom"), "hid"),
        ),
        out_specs=(
            P(("basin", "dom"), "hid"),
            P(("basin", "dom"), "hid"),
            P("basin", "hid"),
            P(("basin", "hid")),
        ),
        check_vma=False,
    )
```
